32 devices in a mesh: groups: 2 (over y), block: 4 (over z), exc: 2 (over x), sub: 2 (over core).
Axes of the slice: x: 2, y: 2, z: 4, core: 2. Of those that a mesh axis runs over, the one named last changes fastest.
Arguments:
- excitation: float32 [8192, 2048], P('block', ('groups', 'exc', 'sub')), parts along dimension 1, may hold values from -6 to 6
- bases: float32 [16, 192, 512], P('block'), may hold values from -0.25 to 0.25
- translations: float32 [2, 192, 192], replicated, may hold values from -0.4375 to 0.4375
- half_order: int32 [2, 192], replicated, may hold values from 0 to 191, each once within a row
- band_offsets: int32 [5], replicated, may hold values from -64 to 64, as said below
- band_coef: float32 [5, 8192], P(None, 'block'), may hold values from -0.6 to 0.6
Outputs:
- applied_twice: float32 [8192, 2048], P('block', ('groups', 'exc', 'sub')), parts along dimension 1
The draws below stay inside these ranges and needn't reach their ends.
There are 2 independent parts, one for each index of `groups`. The reference program is written for one: setup_inputs(seed, part) draws one part's arguments, and reference() takes and returns one part's arrays. A program takes and returns all parts, laid end to end along the dimension named above; an argument that names none is the same for every part. Nothing has to cross between parts.
Inputs may be any that keep to these rules, and one draw needn't show every extreme that they name: `band_offsets`: 5 distinct offsets; both -64 and 64 are among them. `half_order`: each row is a permutation of 0 to 191.
All inputs are finite; a program needn't handle non-finite values.
Results may differ from the reference program's by a relative error of at most 0.0001.
Values sent between devices are 32-bit elements; how exact they have to be, the bound alone decides.
No kernel may reach another device: no remote copies, remote signals or barrier semaphores. Data moves between devices by JAX's collectives and lax.ppermute only.
A program may use at most 64 MiB of HBM per device.

```python
import jax
import jax.numpy as jnp
from jax import lax

LEAF = 512
RANK = 192
NBAND = 5
HALO = 64
LEVELS = 2
TOTAL_LEAVES = 16
ROWS = 8192
COLS = 1024
N_BLOCK = 4


def draw_band_offsets(key, part):
    inner = jax.random.permutation(key, 2 * HALO - 1).astype(jnp.int32) - (HALO - 1)
    selected_option = jnp.concatenate([jnp.array([-HALO, HALO], jnp.int32), inner[:NBAND - 2]])
    shuffle = jax.random.permutation(jax.random.fold_in(key, 7), NBAND)
    return selected_option[shuffle].astype(jnp.int32)


def shard_levels(own_key, extent, cuts, low, high):
    loudness = 1.0
    for axis_at, blocks in cuts:
        steps = jax.random.uniform(jax.random.fold_in(jax.random.fold_in(own_key, 6), axis_at), (blocks,), jnp.float32, low / len(cuts), high / len(cuts))
        loudness = loudness * jnp.repeat(jnp.exp(steps), extent[axis_at] // blocks).reshape((-1,) + (1,) * (len(extent) - 1 - axis_at))
    return loudness


def normal_values(key, dims, width, reach, split=(), dtype=jnp.bfloat16):
    values = jax.random.normal(key, dims, jnp.float32) * width
    if len(split) > 0:
        values = shard_levels(key, dims, split, -0.22, 0.18) * values
    return jnp.clip(values, min=-reach, max=reach).astype(dtype)


def setup_inputs(seed: int = 0, part: int = 0) -> dict:
    streams_of = jax.random.split(jax.random.key(seed), 7)
    part_keys = jax.random.split(jax.random.fold_in(streams_of[6], part), 7)
    excitation = normal_values(part_keys[0], (ROWS, COLS), 1.0, 6.0, ((0, 4), (1, 4)), jnp.float32)
    bases = normal_values(streams_of[1], (TOTAL_LEAVES, RANK, LEAF), LEAF ** -0.5, 0.25, ((0, 4),), jnp.float32)
    translations = normal_values(streams_of[2], (LEVELS, RANK, RANK), RANK ** -0.5, 0.4375, (), jnp.float32)
    half_order = jax.vmap(lambda own: jax.random.permutation(own, RANK))(jax.random.split(streams_of[3], LEVELS)).reshape((LEVELS, RANK)).astype(jnp.int32)
    band_offsets = draw_band_offsets(jax.random.fold_in(streams_of[6], 71), part)
    band_coef = jnp.clip(jax.random.uniform(streams_of[5], (NBAND, ROWS), jnp.float32, -0.6, 0.6) * shard_levels(streams_of[5], (NBAND, ROWS), ((1, 4),), -0.4, 0.0), -0.6, 0.6)
    return dict(excitation=excitation, bases=bases, translations=translations, half_order=half_order, band_offsets=band_offsets, band_coef=band_coef)


TOP_PRECISION = lax.Precision.HIGHEST


def near_field(field, band_offsets, band_coef):
    row_count = field.shape[0]
    padded = jnp.pad(field, ((HALO, HALO), (0, 0)))
    total = jnp.zeros(field.shape, jnp.float32)
    for band_index in range(band_offsets.shape[0]):
        start = (band_offsets[band_index] + HALO).astype(jnp.int32)
        piece = lax.dynamic_slice_in_dim(padded, start, row_count, 0)
        total = total + band_coef[band_index][:, None] * piece
    return total


def far_field(field, bases, translations, half_order):
    leaf_count, rank, leaf_size = bases.shape
    columns = field.shape[1]
    block_list = field.reshape(leaf_count, leaf_size, columns)
    factor_weights = jnp.einsum("bwe,bez->bwz", bases, block_list, precision=TOP_PRECISION)
    group_count = N_BLOCK
    per_group = leaf_count // group_count
    half_rank = rank // 2
    for level_index in range(translations.shape[0]):
        stride = 2 ** level_index
        shaped = factor_weights.reshape(group_count // (2 * stride), 2, stride, per_group, rank, columns)
        partner = jnp.flip(shaped, 1).reshape(factor_weights.shape)
        kept = jnp.take(factor_weights, half_order[level_index, :half_rank], axis=1)
        received = jnp.take(partner, half_order[level_index, half_rank:], axis=1)
        stacked = jnp.concatenate([kept, received], axis=1)
        factor_weights = jnp.einsum("rs,gsc->grc", translations[level_index], stacked, precision=TOP_PRECISION)
    broadened_input = jnp.einsum("npi,npx->nix", bases, factor_weights, precision=TOP_PRECISION)
    return broadened_input.reshape(field.shape)


def apply_integral_operator(field, bases, translations, half_order, band_offsets, band_coef):
    return near_field(field, band_offsets, band_coef) + far_field(field, bases, translations, half_order)


def reference(excitation, bases, translations, half_order, band_offsets, band_coef):
    once = apply_integral_operator(excitation, bases, translations, half_order, band_offsets, band_coef)
    return apply_integral_operator(once, bases, translations, half_order, band_offsets, band_coef)
```

```python
import functools

import jax
import jax.numpy as jnp
from jax import lax
from jax.experimental import pallas as pl
from jax.experimental.pallas import tpu as pltpu
from jax.sharding import PartitionSpec as P

HALO = 64
STRIP = 128
F32 = jnp.float32
BF16 = jnp.bfloat16
LIMIT = 40 * 1024 * 1024

VMEM = pl.BlockSpec(memory_space=pltpu.VMEM)
SMEM = pl.BlockSpec(memory_space=pltpu.SMEM)
ANY = pl.BlockSpec(memory_space=pl.ANY)


def call(body, ins, outs, scratch=(), flops=0, moved=0, aliases=None):
    return pl.pallas_call(
        body,
        in_specs=[s for s, _ in ins],
        out_specs=[s for s, _ in outs],
        out_shape=[jax.ShapeDtypeStruct(*shape) for _, shape in outs],
        scratch_shapes=list(scratch),
        input_output_aliases=aliases or {},
        compiler_params=pltpu.CompilerParams(vmem_limit_bytes=LIMIT),
        cost_estimate=pl.CostEstimate(flops=flops, bytes_accessed=moved, transcendentals=0),
    )(*[a for _, a in ins])


def split(value):
    high = value.astype(BF16)
    return high, (value - high.astype(F32)).astype(BF16)


def dot(a, b, a_dim=1):
    return lax.dot_general(a, b, (((a_dim,), (0,)), ((), ())), preferred_element_type=F32)


def dot3(a, b, a_dim=1):
    return dot(a[0], b[0], a_dim) + (dot(a[0], b[1], a_dim) + dot(a[1], b[0], a_dim))


def picker(order_ref, level, rank):
    row = order_ref[pl.ds(level, 1), :]
    where = lax.broadcasted_iota(jnp.int32, (rank, rank), 0)
    return jnp.where(where == row, 1.0, 0.0).astype(BF16)


def pick(chosen, pair):
    return tuple(dot(chosen, part, 0).astype(BF16) for part in pair)


def head_body(leaf, order, x, bases, kept, send, base_high, base_low, x_buf, base_buf, sems):
    rank, size = base_buf.shape
    half = rank // 2
    base_copy = pltpu.make_async_copy(bases.at[leaf], base_buf, sems.at[0])
    x_copy = pltpu.make_async_copy(x.at[pl.ds(leaf * size, size)], x_buf, sems.at[1])
    base_copy.start()
    x_copy.start()
    chosen = picker(order, 0, rank)
    base_copy.wait()
    base = pick(chosen, split(base_buf[...]))
    base_high[...], base_low[...] = base
    x_copy.wait()
    first = dot3(base, split(x_buf[...]))
    kept[...] = first[:half]
    send[...] = first[half:]


def head(leaf, order, x, bases):
    _, rank, size = bases.shape
    columns = x.shape[1]
    half = ((rank // 2, columns), F32)
    base = ((rank, size), BF16)
    return call(
        functools.partial(head_body, leaf),
        [(VMEM, order), (ANY, x), (ANY, bases)],
        [(VMEM, half), (VMEM, half), (VMEM, base), (VMEM, base)],
        [pltpu.VMEM((size, columns), F32), pltpu.VMEM((rank, size), F32), pltpu.SemaphoreType.DMA((2,))],
        flops=6 * rank * size * columns + 4 * rank * rank * size,
        moved=4 * size * (columns + rank),
    )


def trans_body(order, trans, out_high, out_low):
    levels, rank, _ = trans.shape
    for level in range(levels):
        chosen = picker(order, (level + 1) % levels, rank)
        out_high[level], out_low[level] = pick(chosen, split(trans[level]))


def trans_prep(order, trans):
    shape = (trans.shape, BF16)
    return call(trans_body, [(VMEM, order), (VMEM, trans)], [(VMEM, shape), (VMEM, shape)])


def hop_body(level, kept, received, t_high, t_low, next_kept, next_send):
    half = kept.shape[0]
    stacked = split(jnp.concatenate([kept[...], received[...]], axis=0))
    result = dot3((t_high[level], t_low[level]), stacked)
    next_kept[...] = result[:half]
    next_send[...] = result[half:]


def hop(level, kept, received, trans):
    half = (kept.shape, F32)
    return call(
        functools.partial(hop_body, level),
        [(VMEM, kept), (VMEM, received), (VMEM, trans[0]), (VMEM, trans[1])],
        [(VMEM, half), (VMEM, half)],
        flops=6 * kept.size * 4 * kept.shape[0],
    )


def weight_body(last, base_high, base_low, t_high, t_low, w_high, w_low, m_high, m_low):
    base = (base_high[...], base_low[...])
    w = split(dot3(base, (t_high[last], t_low[last]), 0))
    w_high[...], w_low[...] = w
    m_high[...], m_low[...] = split(dot3(base, w))


def weights(base, trans):
    rank, size = base[0].shape
    w, m = ((size, rank), BF16), ((rank, rank), BF16)
    return call(
        functools.partial(weight_body, trans[0].shape[0] - 1),
        [(VMEM, base[0]), (VMEM, base[1]), (VMEM, trans[0]), (VMEM, trans[1])],
        [(VMEM, w), (VMEM, w), (VMEM, m), (VMEM, m)],
        flops=12 * rank * rank * size,
    )


def band_body(offsets, coef, high, low):
    strips, rows, width = high.shape
    bands = coef.shape[0]
    apart = lax.broadcasted_iota(jnp.int32, (rows, width), 1) - lax.broadcasted_iota(
        jnp.int32, (rows, width), 0
    )
    masks = [apart == offsets[b] + HALO for b in range(bands)]
    padded = jnp.concatenate([coef[...], jnp.zeros((8 - bands, coef.shape[1]), F32)], axis=0)
    for s in range(strips):
        tall = jnp.transpose(padded[:, s * rows : (s + 1) * rows])
        strip = jnp.zeros((rows, width), F32)
        for b in range(bands):
            strip = jnp.where(masks[b], tall[:, b : b + 1], strip)
        high[s], low[s] = split(strip)


def band_prep(offsets, coef):
    shape = ((coef.shape[1] // STRIP, STRIP, STRIP + 2 * HALO), BF16)
    return call(band_body, [(SMEM, offsets), (VMEM, coef)], [(VMEM, shape), (VMEM, shape)])


def extend(field, low, high, buf):
    rows = field.shape[0]
    for at, part in ((0, low[...]), (HALO, field[...]), (HALO + rows, high[...])):
        buf[0, at : at + part.shape[0]], buf[1, at : at + part.shape[0]] = split(part)


def strip_product(band_high, band_low, s, buf):
    rows, width = band_high.shape[1:]
    at = slice(s * rows, s * rows + width)
    return dot3((band_high[s], band_low[s]), (buf[0, at], buf[1, at]))


def near_body(leaves, x, low, high, band_high, band_low, *rest):
    bases, rest = rest[: 2 * leaves], rest[2 * leaves :]
    near, parts, buf = rest[0], rest[1 : 1 + leaves], rest[1 + leaves]
    extend(x, low, high, buf)
    size = x.shape[0] // leaves
    per_leaf = size // STRIP
    for leaf in range(leaves):
        for s in range(leaf * per_leaf, (leaf + 1) * per_leaf):
            near[s * STRIP : (s + 1) * STRIP] = strip_product(band_high, band_low, s, buf)
        base = (bases[2 * leaf][...], bases[2 * leaf + 1][...])
        parts[leaf][...] = dot3(base, split(near[leaf * size : (leaf + 1) * size]))


def near_first(x, low, high, band, bases):
    leaves = len(bases)
    rank = bases[0][0].shape[0]
    rows, columns = x.shape
    flat = [b for base in bases for b in base]
    out = call(
        functools.partial(near_body, leaves),
        [(VMEM, x), (VMEM, low), (VMEM, high), (VMEM, band[0]), (VMEM, band[1])] + [(VMEM, b) for b in flat],
        [(VMEM, (x.shape, F32))] + [(VMEM, ((rank, columns), F32))] * leaves,
        [pltpu.VMEM((2, rows + 2 * HALO, columns), BF16)],
        flops=6 * rows * columns * (rank + 2 * STRIP),
    )
    return out[0], out[1:]


def turn_body(kept, received, part, m_high, m_low, next_kept, next_send):
    half = kept.shape[0]
    stacked = split(jnp.concatenate([kept[...], received[...]], axis=0))
    result = part[...] + dot3((m_high[...], m_low[...]), stacked)
    next_kept[...] = result[:half]
    next_send[...] = result[half:]


def turn(kept, received, part, m):
    half = (kept.shape, F32)
    return call(
        turn_body,
        [(VMEM, a) for a in (kept, received, part, *m)],
        [(VMEM, half)] * 2,
        flops=6 * kept.size * 4 * kept.shape[0],
    )


def once_body(leaves, near, *rest):
    ins, (once, first, last) = rest[: 4 * leaves], rest[4 * leaves :]
    size = near.shape[0] // leaves
    for leaf in range(leaves):
        kept, received, w_high, w_low = ins[4 * leaf : 4 * leaf + 4]
        stacked = split(jnp.concatenate([kept[...], received[...]], axis=0))
        rows = slice(leaf * size, (leaf + 1) * size)
        once[rows] = near[rows] + dot3((w_high[...], w_low[...]), stacked)
    first[...] = once[:HALO]
    last[...] = once[near.shape[0] - HALO :]


def once_all(near, ends, w):
    leaves = len(ends)
    flat = [a for end, pair in zip(ends, w) for a in (*end, *pair)]
    edge = ((HALO, near.shape[1]), F32)
    return call(
        functools.partial(once_body, leaves),
        [(VMEM, near)] + [(VMEM, a) for a in flat],
        [(VMEM, (near.shape, F32)), (VMEM, edge), (VMEM, edge)],
        flops=6 * near.size * 2 * ends[0][0].shape[0],
    )


def again_body(once, low, high, band_high, band_low, near, buf):
    extend(once, low, high, buf)
    for s in range(once.shape[0] // STRIP):
        near[s * STRIP : (s + 1) * STRIP] = strip_product(band_high, band_low, s, buf)


def near_again(once, low, high, band):
    rows, columns = once.shape
    return call(
        again_body,
        [(VMEM, a) for a in (once, low, high, *band)],
        [(VMEM, (once.shape, F32))],
        [pltpu.VMEM((2, rows + 2 * HALO, columns), BF16)],
        flops=6 * once.size * 2 * STRIP,
    )[0]


def tail_body(leaf, *refs):
    near, kept, received, w_high, w_low = refs[:5]
    out, buf, sem = refs[-3:]
    size = w_high.shape[0]
    rows = pl.ds(leaf * size, size)
    stacked = split(jnp.concatenate([kept[...], received[...]], axis=0))
    buf[...] = near[rows] + dot3((w_high[...], w_low[...]), stacked)
    copy = pltpu.make_async_copy(buf, out.at[rows], sem)
    copy.start()
    copy.wait()


def tail(leaf, near, end, w, out):
    ins = [(VMEM, a) for a in (near, *end, *w)]
    if out is not None:
        ins.append((ANY, out))
    size, rank = w[0].shape
    return call(
        functools.partial(tail_body, leaf),
        ins,
        [(ANY, (near.shape, F32))],
        [pltpu.VMEM((size, near.shape[1]), F32), pltpu.SemaphoreType.DMA],
        flops=6 * size * rank * near.shape[1],
        moved=4 * size * near.shape[1],
        aliases={5: 0} if out is not None else None,
    )[0]


def partner(value, level, count):
    return lax.ppermute(value, "block", [(i, i ^ 2**level) for i in range(count)])


def shift(low_edge, high_edge, count):
    forward = [(i, i + 1) for i in range(count - 1)]
    return (
        lax.ppermute(high_edge, "block", forward),
        lax.ppermute(low_edge, "block", [(b, a) for a, b in forward]),
    )


def per_device(x, bases, trans, order, offsets, coef):
    leaves = bases.shape[0]
    rows = x.shape[0]
    count = lax.axis_size("block")
    levels = count.bit_length() - 1

    def cross(kept, send):
        for level in range(levels):
            received = partner(send, level, count)
            if level < levels - 1:
                kept, send = hop(level, kept, received, moves)
        return kept, received

    moves = trans_prep(order, trans)
    heads = [head(leaf, order, x, bases) for leaf in range(leaves)]
    base = [h[2:] for h in heads]
    low, high = shift(x[:HALO], x[rows - HALO :], count)
    band = band_prep(offsets, coef)
    both = [weights(b, moves) for b in base]
    w, m = [b[:2] for b in both], [b[2:] for b in both]
    near, parts = near_first(x, low, high, band, base)
    ends = [cross(*h[:2]) for h in heads]
    turns = [turn(*end, part, pair) for end, part, pair in zip(ends, parts, m)]
    once, first, last = once_all(near, ends, w)
    low, high = shift(first, last, count)
    near = near_again(once, low, high, band)
    ends = [cross(*t) for t in turns]
    out = None
    for leaf in range(leaves):
        out = tail(leaf, near, ends[leaf], w[leaf], out)
    return out


def solution(mesh):
    in_specs = (
        P("block", ("groups", "exc", "sub")),
        P("block", None, None),
        P(),
        P(),
        P(),
        P(None, "block"),
    )
    out_specs = P("block", ("groups", "exc", "sub"))
    return jax.shard_map(
        per_device, mesh=mesh, in_specs=in_specs, out_specs=out_specs, check_vma=False
    )
```

```python
import functools

import jax
import jax.numpy as jnp
from jax import lax
from jax.experimental import pallas as pl
from jax.experimental.pallas import tpu as pltpu
from jax.sharding import PartitionSpec as P

HALO = 64
STRIP = 128
F32 = jnp.float32
BF16 = jnp.bfloat16
LIMIT = 40 * 1024 * 1024

VMEM = pl.BlockSpec(memory_space=pltpu.VMEM)
SMEM = pl.BlockSpec(memory_space=pltpu.SMEM)
HBM = pl.BlockSpec(memory_space=pltpu.HBM)


class Line:
    def __init__(self):
        self.last = None

    def call(self, body, ins, outs, scratch=(), aliases=None, limit=LIMIT):
        values = [a for _, a in ins]
        if self.last is not None:
            *values, _ = lax.optimization_barrier((*values, self.last))
        result = pl.pallas_call(
            body,
            in_specs=[s for s, _ in ins],
            out_specs=[s for s, _ in outs],
            out_shape=[jax.ShapeDtypeStruct(*shape) for _, shape in outs],
            scratch_shapes=list(scratch),
            input_output_aliases=aliases or {},
            compiler_params=pltpu.CompilerParams(vmem_limit_bytes=limit),
            cost_estimate=pl.CostEstimate(flops=1, bytes_accessed=1, transcendentals=0),
        )(*values)
        self.last = result[0]
        return result


def split(value):
    high = value.astype(BF16)
    return high, (value - high.astype(F32)).astype(BF16)


def dot(a, b, a_dim=1):
    return lax.dot_general(a, b, (((a_dim,), (0,)), ((), ())), preferred_element_type=F32)


def dot3(a, b, a_dim=1):
    return dot(a[0], b[0], a_dim) + (dot(a[0], b[1], a_dim) + dot(a[1], b[0], a_dim))


def picker(order_ref, level, rank):
    row = order_ref[pl.ds(level, 1), :]
    where = lax.broadcasted_iota(jnp.int32, (rank, rank), 0)
    return jnp.where(where == row, 1.0, 0.0).astype(BF16)


def pick(chosen, pair):
    return tuple(dot(chosen, part, 0).astype(BF16) for part in pair)


def store_halves(n, result, kept, send):
    half = result.shape[0] // 2
    kept[n * half : (n + 1) * half] = result[:half]
    send[n * half : (n + 1) * half] = result[half:]


def stacked(n, half, kept, received):
    rows = slice(n * half, (n + 1) * half)
    return split(jnp.concatenate([kept[rows], received[rows]], axis=0))


def first_body(leaf, order, x, bases, kept, send, base_high, base_low, x_buf, base_buf, sems):
    rank, size = base_buf.shape
    base_copy = pltpu.make_async_copy(bases.at[leaf], base_buf, sems.at[0])
    x_copy = pltpu.make_async_copy(x.at[pl.ds(leaf * size, size)], x_buf, sems.at[1])
    base_copy.start()
    x_copy.start()
    chosen = picker(order, 0, rank)
    base_copy.wait()
    base = pick(chosen, split(base_buf[...]))
    base_high[0], base_low[0] = base
    x_copy.wait()
    store_halves(0, dot3(base, split(x_buf[...])), kept, send)


def head_body(leaves, order, x, bases, kept, send, base_high, base_low):
    _, rank, size = bases.shape
    chosen = picker(order, 0, rank)
    for n, leaf in enumerate(leaves):
        base = pick(chosen, split(bases[leaf]))
        base_high[n], base_low[n] = base
        store_halves(n, dot3(base, split(x[leaf * size : (leaf + 1) * size])), kept, send)


def head(line, leaves, order, x, bases, first):
    _, rank, size = bases.shape
    columns = x.shape[1]
    half = ((len(leaves) * rank // 2, columns), F32)
    base = ((len(leaves), rank, size), BF16)
    scratch = [pltpu.VMEM((size, columns), F32), pltpu.VMEM((rank, size), F32), pltpu.SemaphoreType.DMA((2,))]
    where = HBM if first else VMEM
    return line.call(
        functools.partial(first_body, leaves[0]) if first else functools.partial(head_body, leaves),
        [(VMEM, order), (where, x), (where, bases)],
        [(VMEM, half), (VMEM, half), (VMEM, base), (VMEM, base)],
        scratch if first else (),
        limit=63 * 1024 * 1024 if first else LIMIT,
    )


def trans_body(order, trans, out_high, out_low):
    levels, rank, _ = trans.shape
    for level in range(levels):
        chosen = picker(order, (level + 1) % levels, rank)
        out_high[level], out_low[level] = pick(chosen, split(trans[level]))


def trans_prep(line, order, trans):
    shape = (trans.shape, BF16)
    return line.call(trans_body, [(VMEM, order), (VMEM, trans)], [(VMEM, shape), (VMEM, shape)])


def hop_body(level, count, kept, received, t_high, t_low, next_kept, next_send):
    half = kept.shape[0] // count
    for n in range(count):
        result = dot3((t_high[level], t_low[level]), stacked(n, half, kept, received))
        store_halves(n, result, next_kept, next_send)


def hop(line, level, count, kept, received, trans):
    half = (kept.shape, F32)
    return line.call(
        functools.partial(hop_body, level, count),
        [(VMEM, kept), (VMEM, received), (VMEM, trans[0]), (VMEM, trans[1])],
        [(VMEM, half), (VMEM, half)],
    )


def band_body(offsets, coef, high, low):
    strips, rows, width = high.shape
    bands = coef.shape[0]
    apart = lax.broadcasted_iota(jnp.int32, (rows, width), 1) - lax.broadcasted_iota(
        jnp.int32, (rows, width), 0
    )
    group = rows // 8
    padded = jnp.concatenate([coef[...], jnp.zeros((8 - bands, coef.shape[1]), F32)], axis=0)
    for start in range(0, strips, group):
        here = range(start, min(start + group, strips))
        parts = [padded[:, s * rows : (s + 1) * rows] for s in here]
        parts += [jnp.zeros((8, rows), F32)] * (group - len(parts))
        tall = jnp.transpose(jnp.concatenate(parts, axis=0))
        for n, s in enumerate(here):
            strip = jnp.zeros((rows, width), F32)
            for b in range(bands):
                at = n * 8 + b
                strip = jnp.where(apart == offsets[b] + HALO, tall[:, at : at + 1], strip)
            high[s], low[s] = split(strip)


def band_prep(line, offsets, coef):
    shape = ((coef.shape[1] // STRIP, STRIP, STRIP + 2 * HALO), BF16)
    return line.call(band_body, [(SMEM, offsets), (VMEM, coef)], [(VMEM, shape), (VMEM, shape)])


def near_body(count, low, *refs):
    parts = refs[:count]
    high, band_high, band_low, near, buf = refs[count:]
    at = 0
    for part in (low, *parts, high):
        rows = slice(at, at + part.shape[0])
        buf[0, rows], buf[1, rows] = split(part[...])
        at += part.shape[0]
    width = band_high.shape[2]
    for s in range(band_high.shape[0]):
        rows = slice(s * STRIP, s * STRIP + width)
        near[s * STRIP : (s + 1) * STRIP] = dot3(
            (band_high[s], band_low[s]), (buf[0, rows], buf[1, rows])
        )


def near_field(line, parts, low, high, band):
    rows = sum(p.shape[0] for p in parts)
    columns = low.shape[1]
    return line.call(
        functools.partial(near_body, len(parts)),
        [(VMEM, a) for a in (low, *parts, high, *band)],
        [(VMEM, ((rows, columns), F32))],
        [pltpu.VMEM((2, rows + 2 * HALO, columns), BF16)],
    )[0]


def finished(n, half, kept, received, t_high, t_low, base_high, base_low, near):
    final = t_high.shape[0] - 1
    last = split(dot3((t_high[final], t_low[final]), stacked(n, half, kept, received)))
    return near + dot3((base_high[n], base_low[n]), last, 0)


def turn_body(start, count, near, kept, received, t_high, t_low, base_high, base_low, next_kept, next_send, once):
    half = kept.shape[0] // count
    size = base_high.shape[2]
    for n in range(count):
        rows = slice(start + n * size, start + (n + 1) * size)
        field = finished(n, half, kept, received, t_high, t_low, base_high, base_low, near[rows])
        once[n * size : (n + 1) * size] = field
        result = dot3((base_high[n], base_low[n]), split(field))
        store_halves(n, result, next_kept, next_send)


def turn(line, leaves, near, end, trans, base):
    half = (end[0].shape, F32)
    size = base[0].shape[2]
    return line.call(
        functools.partial(turn_body, leaves[0] * size, len(leaves)),
        [(VMEM, a) for a in (near, *end, *trans, *base)],
        [(VMEM, half), (VMEM, half), (VMEM, ((len(leaves) * size, near.shape[1]), F32))],
    )


def tail_body(start, count, *refs):
    near, kept, received, t_high, t_low, base_high, base_low = refs[:7]
    out, buf, sem = refs[-3:]
    half = kept.shape[0] // count
    size = base_high.shape[2]
    copies = []
    for n in range(count):
        rows = slice(start + n * size, start + (n + 1) * size)
        buf[n] = finished(n, half, kept, received, t_high, t_low, base_high, base_low, near[rows])
        copies.append(pltpu.make_async_copy(buf.at[n], out.at[pl.ds(start + n * size, size)], sem.at[n]))
        copies[-1].start()
    for copy in copies:
        copy.wait()


def tail(line, leaves, near, end, trans, base, out):
    ins = [(VMEM, a) for a in (near, *end, *trans, *base)]
    if out is not None:
        ins.append((HBM, out))
    size = base[0].shape[2]
    return line.call(
        functools.partial(tail_body, leaves[0] * size, len(leaves)),
        ins,
        [(HBM, (near.shape, F32))],
        [pltpu.VMEM((len(leaves), size, near.shape[1]), F32), pltpu.SemaphoreType.DMA((len(leaves),))],
        aliases={7: 0} if out is not None else None,
    )[0]


def partner(value, level, count):
    return lax.ppermute(value, "block", [(i, i ^ 2**level) for i in range(count)])


def shift(low_edge, high_edge, count):
    forward = [(i, i + 1) for i in range(count - 1)]
    return (
        lax.ppermute(high_edge, "block", forward),
        lax.ppermute(low_edge, "block", [(b, a) for a, b in forward]),
    )


def chunks_of(leaves):
    return [(leaf,) for leaf in range(leaves)]


def per_device(x, bases, trans, order, offsets, coef):
    rows = x.shape[0]
    count = lax.axis_size("block")
    levels = count.bit_length() - 1
    chunks = chunks_of(bases.shape[0])
    final = len(chunks) - 1
    line = Line()
    state, base = {}, {}
    moves = None

    def begin(c):
        kept, send, *base[c] = head(line, chunks[c], order, x, bases, c == 0)
        state[c] = kept, partner(send, 0, count)

    def step(c, level):
        kept, send = hop(line, level, len(chunks[c]), *state[c], moves)
        state[c] = kept, partner(send, level + 1, count)

    low, high = shift(x[:HALO], x[rows - HALO :], count)
    begin(0)
    begin(1)
    moves = trans_prep(line, order, trans)
    for level in range(levels - 1):
        for c in range(final + 1):
            step(c, level)
            if level == 0 and c + 2 <= final:
                begin(c + 2)
    band = band_prep(line, offsets, coef)
    near = near_field(line, [x], low, high, band)
    once = {}

    def turn_at(c):
        kept, send, once[c] = turn(line, chunks[c], near, state[c], moves, base[c])
        state[c] = kept, partner(send, 0, count)

    turn_at(0)
    for c in range(1, final + 1):
        turn_at(c)
        if levels > 1:
            step(c - 1, 0)
    low, high = shift(once[0][:HALO], once[final][once[final].shape[0] - HALO :], count)
    if levels > 1:
        step(final, 0)
    for level in range(1, levels - 1):
        for c in range(final + 1):
            step(c, level)
    near = near_field(line, [once[c] for c in range(final + 1)], low, high, band)
    out = None
    for c in range(final + 1):
        out = tail(line, chunks[c], near, state[c], moves, base[c], out)
    return out


def solution(mesh):
    in_specs = (
        P("block", ("groups", "exc", "sub")),
        P("block", None, None),
        P(),
        P(),
        P(),
        P(None, "block"),
    )
    out_specs = P("block", ("groups", "exc", "sub"))
    return jax.shard_map(
        per_device, mesh=mesh, in_specs=in_specs, out_specs=out_specs, check_vma=False
    )
```

```python
import functools

import jax
import jax.numpy as jnp
from jax import lax
from jax.experimental import pallas as pl
from jax.experimental.pallas import tpu as pltpu
from jax.sharding import PartitionSpec as P

HALO = 64
STRIP = 128
F32 = jnp.float32
BF16 = jnp.bfloat16
LIMIT = 24 * 1024 * 1024

VMEM = pl.BlockSpec(memory_space=pltpu.VMEM)
SMEM = pl.BlockSpec(memory_space=pltpu.SMEM)
HBM = pl.BlockSpec(memory_space=pltpu.HBM)


class Line:
    def __init__(self):
        self.last = None

    def call(self, body, ins, outs, scratch=(), aliases=None, cost=1.0):
        values = [a for _, a in ins]
        if self.last is not None:
            *values, _ = lax.optimization_barrier((*values, self.last))
        placed = [
            a if s is SMEM else pltpu.with_memory_space_constraint(a, s.memory_space)
            for (s, _), a in zip(ins, values)
        ]
        result = pl.pallas_call(
            body,
            in_specs=[s for s, _ in ins],
            out_specs=[s for s, _ in outs],
            out_shape=[s.memory_space(*shape) for s, shape in outs],
            scratch_shapes=list(scratch),
            input_output_aliases=aliases or {},
            compiler_params=pltpu.CompilerParams(vmem_limit_bytes=LIMIT),
            cost_estimate=pl.CostEstimate(
                flops=int(cost * 1e9), bytes_accessed=int(cost * 3e6), transcendentals=0
            ),
        )(*placed)
        self.last = result[0]
        return result


def split(value):
    high = value.astype(BF16)
    return high, (value - high.astype(F32)).astype(BF16)


def dot(a, b, a_dim=1):
    return lax.dot_general(a, b, (((a_dim,), (0,)), ((), ())), preferred_element_type=F32)


def dot3(a, b, a_dim=1):
    return dot(a[0], b[0], a_dim) + (dot(a[0], b[1], a_dim) + dot(a[1], b[0], a_dim))


def picker(order_ref, level, rank):
    row = order_ref[pl.ds(level, 1), :]
    where = lax.broadcasted_iota(jnp.int32, (rank, rank), 0)
    return jnp.where(where == row, 1.0, 0.0).astype(BF16)


def pick(chosen, pair):
    return tuple(dot(chosen, part, 0).astype(BF16) for part in pair)


def store_halves(n, result, kept, send):
    half = result.shape[0] // 2
    kept[n * half : (n + 1) * half] = result[:half]
    send[n * half : (n + 1) * half] = result[half:]


def stacked(n, half, kept, received):
    rows = slice(n * half, (n + 1) * half)
    return split(jnp.concatenate([kept[rows], received[rows]], axis=0))


def head_leaves(n, base, x, kept, send, base_high, base_low):
    base_high[n], base_low[n] = base
    store_halves(n, dot3(base, split(x)), kept, send)


def first_body(leaves, parity, order, x, bases, kept, send, base_high, base_low, across, x_all, bases_all, order_buf, sems):
    _, rank, size = bases.shape
    rows, columns = x.shape
    split_at = len(leaves) * size
    copies = [
        pltpu.make_async_copy(a, b, sems.at[n])
        for n, (a, b) in enumerate(
            (
                (order, order_buf),
                (bases.at[pl.ds(0, len(leaves))], bases_all.at[pl.ds(0, len(leaves))]),
                (x.at[pl.ds(0, split_at)], x_all.at[pl.ds(0, split_at)]),
                (x.at[pl.ds(split_at, rows - split_at)], x_all.at[pl.ds(split_at, rows - split_at)]),
                (
                    bases.at[pl.ds(len(leaves), bases.shape[0] - len(leaves))],
                    bases_all.at[pl.ds(len(leaves), bases.shape[0] - len(leaves))],
                ),
            )
        )
    ]
    for copy in copies:
        copy.start()
    copies[0].wait()
    chosen = picker(order_buf, 0, rank)
    copies[1].wait()
    picked = [pick(chosen, split(bases_all[leaf])) for leaf in leaves]
    copies[2].wait()
    for n, leaf in enumerate(leaves):
        head_leaves(n, picked[n], x_all[leaf * size : (leaf + 1) * size], kept, send, base_high, base_low)
    copies[3].wait()
    edges(parity, x_all, send, across)
    copies[4].wait()


def edges(parity, field, send, across):
    rows = field.shape[0]
    even = jnp.full((HALO, field.shape[1]), parity[0], jnp.int32) == 0
    first, last = field[:HALO], field[rows - HALO :]
    send[send.shape[0] - HALO :] = jnp.where(even, last, first)
    across[...] = jnp.where(even, first, last)


def head_body(leaves, order, x, bases, kept, send, base_high, base_low):
    _, rank, size = bases.shape
    chosen = picker(order, 0, rank)
    for n, leaf in enumerate(leaves):
        base = pick(chosen, split(bases[leaf]))
        head_leaves(n, base, x[leaf * size : (leaf + 1) * size], kept, send, base_high, base_low)


def head_outs(leaves, x, bases, extra):
    _, rank, size = bases.shape
    half = len(leaves) * rank // 2
    base = ((len(leaves), rank, size), BF16)
    return [
        (VMEM, ((half, x.shape[1]), F32)),
        (VMEM, ((half + extra, x.shape[1]), F32)),
        (VMEM, base),
        (VMEM, base),
    ]


def first_head(line, leaves, parity, order, x, bases, cost):
    return line.call(
        functools.partial(first_body, leaves),
        [(SMEM, parity), (HBM, order), (HBM, x), (HBM, bases)],
        head_outs(leaves, x, bases, HALO)
        + [(VMEM, ((HALO, x.shape[1]), F32)), (VMEM, (x.shape, F32)), (VMEM, (bases.shape, F32))],
        [pltpu.VMEM(order.shape, jnp.int32), pltpu.SemaphoreType.DMA((5,))],
        cost=cost,
    )


def head(line, leaves, order, x, bases, cost):
    return line.call(
        functools.partial(head_body, leaves),
        [(VMEM, order), (VMEM, x), (VMEM, bases)],
        head_outs(leaves, x, bases, 0),
        cost=cost,
    )


def trans_body(order, trans, out_high, out_low):
    levels, rank, _ = trans.shape
    for level in range(levels):
        chosen = picker(order, (level + 1) % levels, rank)
        out_high[level], out_low[level] = pick(chosen, split(trans[level]))


def trans_prep(line, order, trans, cost):
    shape = (trans.shape, BF16)
    return line.call(trans_body, [(VMEM, order), (VMEM, trans)], [(VMEM, shape), (VMEM, shape)], cost=cost)


def hop_body(level, count, kept, received, t_high, t_low, next_kept, next_send):
    half = kept.shape[0] // count
    for n in range(count):
        result = dot3((t_high[level], t_low[level]), stacked(n, half, kept, received))
        store_halves(n, result, next_kept, next_send)


def hop(line, level, count, kept, received, trans, cost):
    half = (kept.shape, F32)
    return line.call(
        functools.partial(hop_body, level, count),
        [(VMEM, kept), (VMEM, received), (VMEM, trans[0]), (VMEM, trans[1])],
        [(VMEM, half), (VMEM, half)],
        cost=cost,
    )


def band_body(offsets, coef, high, low):
    strips, rows, width = high.shape
    bands = coef.shape[0]
    apart = lax.broadcasted_iota(jnp.int32, (rows, width), 1) - lax.broadcasted_iota(
        jnp.int32, (rows, width), 0
    )
    group = rows // 8
    padded = jnp.concatenate([coef[...], jnp.zeros((8 - bands, coef.shape[1]), F32)], axis=0)
    for start in range(0, strips, group):
        here = range(start, min(start + group, strips))
        parts = [padded[:, s * rows : (s + 1) * rows] for s in here]
        parts += [jnp.zeros((8, rows), F32)] * (group - len(parts))
        tall = jnp.transpose(jnp.concatenate(parts, axis=0))
        for n, s in enumerate(here):
            strip = jnp.zeros((rows, width), F32)
            for b in range(bands):
                at = n * 8 + b
                strip = jnp.where(apart == offsets[b] + HALO, tall[:, at : at + 1], strip)
            high[s], low[s] = split(strip)


def band_prep(line, offsets, coef, cost):
    shape = ((coef.shape[1] // STRIP, STRIP, STRIP + 2 * HALO), BF16)
    return line.call(band_body, [(SMEM, offsets), (VMEM, coef)], [(VMEM, shape), (VMEM, shape)], cost=cost)


def extend(parity, near_edge, far_edge, fields, buf):
    at = HALO
    for field in fields:
        rows = slice(at, at + field.shape[0])
        buf[0, rows], buf[1, rows] = split(field[...])
        at += field.shape[0]
    even = jnp.full(far_edge.shape, parity[0], jnp.int32) == 0
    from_partner = near_edge[near_edge.shape[0] - HALO :]
    buf[0, :HALO], buf[1, :HALO] = split(jnp.where(even, far_edge[...], from_partner))
    buf[0, at:], buf[1, at:] = split(jnp.where(even, from_partner, far_edge[...]))


def strip_product(band_high, band_low, s, buf):
    rows = slice(s * STRIP, s * STRIP + band_high.shape[2])
    return dot3((band_high[s], band_low[s]), (buf[0, rows], buf[1, rows]))


def near_body(parity, near_edge, far_edge, field, band_high, band_low, near, buf):
    extend(parity, near_edge, far_edge, [field], buf)
    for s in range(band_high.shape[0]):
        near[s * STRIP : (s + 1) * STRIP] = strip_product(band_high, band_low, s, buf)


def near_field(line, parity, field, near_edge, far_edge, band, cost):
    rows, columns = field.shape
    return line.call(
        near_body,
        [(SMEM, parity)] + [(VMEM, a) for a in (near_edge, far_edge, field, *band)],
        [(VMEM, ((rows, columns), F32))],
        [pltpu.VMEM((2, rows + 2 * HALO, columns), BF16)],
        cost=cost,
    )[0]


def far_rows(n, half, kept, received, t_high, t_low, base_high, base_low):
    final = t_high.shape[0] - 1
    last = split(dot3((t_high[final], t_low[final]), stacked(n, half, kept, received)))
    return dot3((base_high[n], base_low[n]), last, 0)


def finished(n, half, kept, received, t_high, t_low, base_high, base_low, near):
    return near + far_rows(n, half, kept, received, t_high, t_low, base_high, base_low)


def turn_body(start, count, near, kept, received, t_high, t_low, base_high, base_low, next_kept, next_send, once):
    half = kept.shape[0] // count
    size = base_high.shape[2]
    for n in range(count):
        rows = slice(start + n * size, start + (n + 1) * size)
        field = finished(n, half, kept, received, t_high, t_low, base_high, base_low, near[rows])
        once[n * size : (n + 1) * size] = field
        result = dot3((base_high[n], base_low[n]), split(field))
        store_halves(n, result, next_kept, next_send)


def last_turn_body(start, count, parity, first, *refs):
    *refs, across = refs
    turn_body(start, count, *refs)
    next_send, once = refs[-2:]
    even = jnp.full(across.shape, parity[0], jnp.int32) == 0
    low, high = first[:HALO], once[once.shape[0] - HALO :]
    next_send[next_send.shape[0] - HALO :] = jnp.where(even, high, low)
    across[...] = jnp.where(even, low, high)


def turn(line, leaves, near, end, trans, base, last, cost):
    kept = end[0].shape
    size = base[0].shape[2]
    columns = near.shape[1]
    sent = kept if last is None else (kept[0] + HALO, columns)
    body = turn_body if last is None else last_turn_body
    extra = [] if last is None else [(SMEM, last[0]), (VMEM, last[1])]
    return line.call(
        functools.partial(body, leaves[0] * size, len(leaves)),
        extra + [(VMEM, a) for a in (near, *end, *trans, *base)],
        [(VMEM, (kept, F32)), (VMEM, (sent, F32)), (VMEM, ((len(leaves) * size, columns), F32))]
        + ([] if last is None else [(VMEM, ((HALO, columns), F32))]),
        cost=cost,
    )


def far_body(count, kept, received, t_high, t_low, base_high, base_low, far):
    half = kept.shape[0] // count
    size = base_high.shape[2]
    for n in range(count):
        rows = slice(n * size, (n + 1) * size)
        far[rows] = far_rows(n, half, kept, received, t_high, t_low, base_high, base_low)


def far_field(line, leaves, end, trans, base, cost):
    shape = (len(leaves) * base[0].shape[2], end[0].shape[1])
    return line.call(
        functools.partial(far_body, len(leaves)),
        [(VMEM, a) for a in (*end, *trans, *base)],
        [(VMEM, (shape, F32))],
        cost=cost,
    )[0]


def put(copies, value, start, buf, out, sems):
    n = len(copies)
    buf[n] = value
    copies.append(pltpu.make_async_copy(buf.at[n], out.at[pl.ds(start, buf.shape[1])], sems.at[n]))
    copies[-1].start()


def near_again_body(parts, done, size, parity, near_edge, far_edge, *refs):
    fields, refs = refs[:parts], refs[parts:]
    (band_high, band_low), fars = refs[:2], refs[2 : 2 + done]
    out, near, buf, result, sems = refs[2 + done :]
    extend(parity, near_edge, far_edge, fields, buf)
    copies, at, per = [], 0, size // STRIP
    for far in fars:
        for leaf in range(far.shape[0] // size):
            strips = [
                strip_product(band_high, band_low, s, buf)
                for s in range(at // STRIP, at // STRIP + per)
            ]
            value = jnp.concatenate(strips, axis=0) + far[leaf * size : (leaf + 1) * size]
            put(copies, value, at, result, out, sems)
            at += size
    for s in range(at // STRIP, band_high.shape[0]):
        near[s * STRIP - at : (s + 1) * STRIP - at] = strip_product(band_high, band_low, s, buf)
    for copy in copies:
        copy.wait()


def near_again(line, parity, fields, near_edge, far_edge, band, fars, size, cost):
    columns = far_edge.shape[1]
    rows = sum(f.shape[0] for f in fields)
    ready = sum(f.shape[0] for f in fars)
    return line.call(
        functools.partial(near_again_body, len(fields), len(fars), size),
        [(SMEM, parity)] + [(VMEM, a) for a in (near_edge, far_edge, *fields, *band, *fars)],
        [(HBM, ((rows, columns), F32)), (VMEM, ((rows - ready, columns), F32))],
        [
            pltpu.VMEM((2, rows + 2 * HALO, columns), BF16),
            pltpu.VMEM((ready // size, size, columns), F32),
            pltpu.SemaphoreType.DMA((ready // size,)),
        ],
        cost=cost,
    )


def tail_body(start, skip, count, near, kept, received, t_high, t_low, base_high, base_low, _, out, buf, sems):
    half = kept.shape[0] // count
    size = base_high.shape[2]
    copies = []
    for n in range(count):
        rows = slice(start - skip + n * size, start - skip + (n + 1) * size)
        field = finished(n, half, kept, received, t_high, t_low, base_high, base_low, near[rows])
        put(copies, field, start + n * size, buf, out, sems)
    for copy in copies:
        copy.wait()


def tail(line, leaves, near, end, trans, base, out, cost):
    size = base[0].shape[2]
    return line.call(
        functools.partial(tail_body, leaves[0] * size, out.shape[0] - near.shape[0], len(leaves)),
        [(VMEM, a) for a in (near, *end, *trans, *base)] + [(HBM, out)],
        [(HBM, (out.shape, F32))],
        [pltpu.VMEM((len(leaves), size, near.shape[1]), F32), pltpu.SemaphoreType.DMA((len(leaves),))],
        aliases={7: 0},
        cost=cost,
    )[0]


def partner(value, level, count):
    return lax.ppermute(value, "block", [(i, i ^ 2**level) for i in range(count)])


def other_side(edge, count):
    pairs = [(i, i + 1) for i in range(1, count - 1, 2)]
    return lax.ppermute(edge, "block", pairs + [(b, a) for a, b in pairs])


COST = {"H": 0.5, "P": 0.1, "h": 0.5, "B": 0.1, "N": 0.1, "T": 0.5, "F": 0.5, "A": 0.1, "E": 0.5}


def plan(chunks, levels):
    stages = [("H", 0)] + [("h", level) for level in range(levels - 1)] + [("T", 0)]
    stages += [("g", level) for level in range(levels - 1)] + [("E", 0)]
    events = []
    for c in range(chunks):
        for s, (kind, level) in enumerate(stages):
            events.append((2 * s + c, -s, kind, c, level))
    return [e[2:] for e in sorted(events)]


def per_device(x, bases, trans, order, offsets, coef):
    count = lax.axis_size("block")
    levels = count.bit_length() - 1
    size = bases.shape[2]
    chunks = [(leaf,) for leaf in range(bases.shape[0])]
    final = len(chunks) - 1
    parity = jnp.reshape(lax.axis_index("block") % 2, (1,)).astype(jnp.int32)
    line = Line()
    state, base, once, fars = {}, {}, {}, []
    moves = band = near = out = None
    for kind, c, level in plan(len(chunks), levels):
        if kind == "H":
            if c == 0:
                kept, send, high, low, across, x, bases = first_head(
                    line, chunks[0], parity, order, x, bases, COST["H"]
                )
            else:
                kept, send, high, low = head(line, chunks[c], order, x, bases, COST["H"])
            base[c] = high, low
            state[c] = kept, partner(send, 0, count)
            if c == 0:
                near_edge = state[0][1]
        elif kind in "hg":
            if moves is None:
                moves = trans_prep(line, order, trans, COST["P"])
            kept, send = hop(line, level, len(chunks[c]), *state[c], moves, COST["h"])
            state[c] = kept, partner(send, level + 1, count)
        elif kind == "T":
            if c == 0:
                far_edge = other_side(across, count)
                band = band_prep(line, offsets, coef, COST["B"])
                near = near_field(line, parity, x, near_edge, far_edge, band, COST["N"])
            last = (parity, once[0]) if c == final else None
            kept, send, once[c], *across = turn(line, chunks[c], near, state[c], moves, base[c], last, COST["T"])
            state[c] = kept, partner(send, 0, count)
            if c == final:
                near_edge, far_edge = state[c][1], other_side(across[0], count)
        elif c < 2:
            fars.append(far_field(line, chunks[c], state[c], moves, base[c], COST["F"]))
        else:
            if out is None:
                fields = [once[i] for i in range(final + 1)]
                out, near = near_again(line, parity, fields, near_edge, far_edge, band, fars, size, COST["A"])
            out = tail(line, chunks[c], near, state[c], moves, base[c], out, COST["E"])
    return out


def solution(mesh):
    in_specs = (
        P("block", ("groups", "exc", "sub")),
        P("block", None, None),
        P(),
        P(),
        P(),
        P(None, "block"),
    )
    out_specs = P("block", ("groups", "exc", "sub"))
    return jax.shard_map(
        per_device, mesh=mesh, in_specs=in_specs, out_specs=out_specs, check_vma=False
    )
```

```python
import functools

import jax
import jax.numpy as jnp
from jax import lax
from jax.experimental import pallas as pl
from jax.experimental.pallas import tpu as pltpu
from jax.sharding import PartitionSpec as P

HALO = 64
STRIP = 128
F32 = jnp.float32
BF16 = jnp.bfloat16
LIMIT = 16 * 1024 * 1024

VMEM = pl.BlockSpec(memory_space=pltpu.VMEM)
SMEM = pl.BlockSpec(memory_space=pltpu.SMEM)
HBM = pl.BlockSpec(memory_space=pltpu.HBM)


class Line:
    def __init__(self):
        self.last = None

    def call(self, body, ins, outs, scratch=(), aliases=None, cost=1.0):
        values = [a for _, a in ins]
        if self.last is not None:
            *values, _ = lax.optimization_barrier((*values, self.last))
        placed = [
            a if s is SMEM else pltpu.with_memory_space_constraint(a, s.memory_space)
            for (s, _), a in zip(ins, values)
        ]
        result = pl.pallas_call(
            body,
            in_specs=[s for s, _ in ins],
            out_specs=[s for s, _ in outs],
            out_shape=[s.memory_space(*shape) for s, shape in outs],
            scratch_shapes=list(scratch),
            input_output_aliases=aliases or {},
            compiler_params=pltpu.CompilerParams(vmem_limit_bytes=LIMIT),
            cost_estimate=pl.CostEstimate(
                flops=int(cost * 1e9), bytes_accessed=int(cost * 3e6), transcendentals=0
            ),
        )(*placed)
        self.last = result[0]
        return result


def split(value):
    high = value.astype(BF16)
    return high, (value - high.astype(F32)).astype(BF16)


def dot(a, b, a_dim=1):
    return lax.dot_general(a, b, (((a_dim,), (0,)), ((), ())), preferred_element_type=F32)


def dot3(a, b, a_dim=1):
    return dot(a[0], b[0], a_dim) + (dot(a[0], b[1], a_dim) + dot(a[1], b[0], a_dim))


def picker(order_ref, level, rank):
    row = order_ref[pl.ds(level, 1), :]
    where = lax.broadcasted_iota(jnp.int32, (rank, rank), 0)
    return jnp.where(where == row, 1.0, 0.0).astype(BF16)


def pick(chosen, pair):
    return tuple(dot(chosen, part, 0).astype(BF16) for part in pair)


def store_halves(n, result, kept, send):
    half = result.shape[0] // 2
    kept[n * half : (n + 1) * half] = result[:half]
    send[n * half : (n + 1) * half] = result[half:]


def stacked(n, half, kept, received):
    rows = slice(n * half, (n + 1) * half)
    return split(jnp.concatenate([kept[rows], received[rows]], axis=0))


def head_leaves(n, base, x, kept, send, base_high, base_low):
    base_high[n], base_low[n] = base
    store_halves(n, dot3(base, split(x)), kept, send)


def first_body(leaves, parity, order, x, bases, kept, send, base_high, base_low, across, x_all, bases_all, order_buf, sems):
    _, rank, size = bases.shape
    count = len(leaves)
    ahead, behind = pl.ds(0, count), pl.ds(count, bases.shape[0] - count)
    x_ahead, x_behind = pl.ds(0, count * size), pl.ds(count * size, x.shape[0] - count * size)
    copies = [
        pltpu.make_async_copy(source, target, sems.at[n])
        for n, (source, target) in enumerate(
            (
                (order, order_buf),
                (bases.at[ahead], bases_all.at[ahead]),
                (x.at[x_ahead], x_all.at[x_ahead]),
                (x.at[x_behind], x_all.at[x_behind]),
                (bases.at[behind], bases_all.at[behind]),
            )
        )
    ]
    for copy in copies:
        copy.start()
    copies[0].wait()
    chosen = picker(order_buf, 0, rank)
    copies[1].wait()
    picked = [pick(chosen, split(bases_all[leaf])) for leaf in leaves]
    copies[2].wait()
    for n, leaf in enumerate(leaves):
        head_leaves(n, picked[n], x_all[leaf * size : (leaf + 1) * size], kept, send, base_high, base_low)
    copies[3].wait()
    edges(parity, x_all[:HALO], x_all[x.shape[0] - HALO :], send, across)
    copies[4].wait()


def edges(parity, first, last, send, across):
    even = jnp.full(first.shape, parity[0], jnp.int32) == 0
    send[send.shape[0] - HALO :] = jnp.where(even, last, first)
    across[...] = jnp.where(even, first, last)


def head_body(leaves, order, x, bases, kept, send, base_high, base_low):
    _, rank, size = bases.shape
    chosen = picker(order, 0, rank)
    for n, leaf in enumerate(leaves):
        base = pick(chosen, split(bases[leaf]))
        head_leaves(n, base, x[leaf * size : (leaf + 1) * size], kept, send, base_high, base_low)


def head_outs(leaves, x, bases, extra):
    _, rank, size = bases.shape
    half = len(leaves) * rank // 2
    base = ((len(leaves), rank, size), BF16)
    return [
        (VMEM, ((half, x.shape[1]), F32)),
        (VMEM, ((half + extra, x.shape[1]), F32)),
        (VMEM, base),
        (VMEM, base),
    ]


def first_head(line, leaves, parity, order, x, bases, cost):
    return line.call(
        functools.partial(first_body, leaves),
        [(SMEM, parity), (HBM, order), (HBM, x), (HBM, bases)],
        head_outs(leaves, x, bases, HALO)
        + [(VMEM, ((HALO, x.shape[1]), F32)), (VMEM, (x.shape, F32)), (VMEM, (bases.shape, F32))],
        [pltpu.VMEM(order.shape, jnp.int32), pltpu.SemaphoreType.DMA((5,))],
        cost=cost,
    )


def head(line, leaves, order, x, bases, cost):
    return line.call(
        functools.partial(head_body, leaves),
        [(VMEM, order), (VMEM, x), (VMEM, bases)],
        head_outs(leaves, x, bases, 0),
        cost=cost,
    )


def trans_body(order, trans, out_high, out_low):
    levels, rank, _ = trans.shape
    for level in range(levels):
        chosen = picker(order, (level + 1) % levels, rank)
        out_high[level], out_low[level] = pick(chosen, split(trans[level]))


def trans_prep(line, order, trans, cost):
    shape = (trans.shape, BF16)
    return line.call(trans_body, [(VMEM, order), (VMEM, trans)], [(VMEM, shape), (VMEM, shape)], cost=cost)


def hop_body(level, count, kept, received, t_high, t_low, next_kept, next_send):
    half = kept.shape[0] // count
    for n in range(count):
        result = dot3((t_high[level], t_low[level]), stacked(n, half, kept, received))
        store_halves(n, result, next_kept, next_send)


def hop(line, level, count, kept, received, trans, cost):
    return line.call(
        functools.partial(hop_body, level, count),
        [(VMEM, kept), (VMEM, received), (VMEM, trans[0]), (VMEM, trans[1])],
        [(VMEM, (kept.shape, F32)), (VMEM, (kept.shape, F32))],
        cost=cost,
    )


def band_body(offsets, coef, high, low):
    strips, rows, width = high.shape
    bands = coef.shape[0]
    apart = lax.broadcasted_iota(jnp.int32, (rows, width), 1) - lax.broadcasted_iota(
        jnp.int32, (rows, width), 0
    )
    group = rows // 8
    padded = jnp.concatenate([coef[...], jnp.zeros((8 - bands, coef.shape[1]), F32)], axis=0)
    for start in range(0, strips, group):
        here = range(start, min(start + group, strips))
        parts = [padded[:, s * rows : (s + 1) * rows] for s in here]
        parts += [jnp.zeros((8, rows), F32)] * (group - len(parts))
        tall = jnp.transpose(jnp.concatenate(parts, axis=0))
        for n, s in enumerate(here):
            strip = jnp.zeros((rows, width), F32)
            for b in range(bands):
                at = n * 8 + b
                strip = jnp.where(apart == offsets[b] + HALO, tall[:, at : at + 1], strip)
            high[s], low[s] = split(strip)


def band_prep(line, offsets, coef, cost):
    shape = ((coef.shape[1] // STRIP, STRIP, STRIP + 2 * HALO), BF16)
    return line.call(band_body, [(SMEM, offsets), (VMEM, coef)], [(VMEM, shape), (VMEM, shape)], cost=cost)


def extend(parity, near_edge, far_edge, fields, buf):
    at = HALO
    for field in fields:
        rows = slice(at, at + field.shape[0])
        buf[0, rows], buf[1, rows] = split(field[...])
        at += field.shape[0]
    from_partner, from_other = near_edge[near_edge.shape[0] - HALO :], far_edge[...]
    even = jnp.full(from_other.shape, parity[0], jnp.int32) == 0
    buf[0, :HALO], buf[1, :HALO] = split(jnp.where(even, from_other, from_partner))
    buf[0, at:], buf[1, at:] = split(jnp.where(even, from_partner, from_other))


def strip_product(band_high, band_low, s, buf):
    rows = slice(s * STRIP, s * STRIP + band_high.shape[2])
    return dot3((band_high[s], band_low[s]), (buf[0, rows], buf[1, rows]))


def near_body(parity, near_edge, far_edge, field, band_high, band_low, near, buf):
    extend(parity, near_edge, far_edge, [field], buf)
    for s in range(band_high.shape[0]):
        near[s * STRIP : (s + 1) * STRIP] = strip_product(band_high, band_low, s, buf)


def near_field(line, parity, field, halo, band, cost):
    rows, columns = field.shape
    return line.call(
        near_body,
        [(SMEM, parity)] + [(VMEM, a) for a in (*halo, field, *band)],
        [(VMEM, ((rows, columns), F32))],
        [pltpu.VMEM((2, rows + 2 * HALO, columns), BF16)],
        cost=cost,
    )[0]


def far_rows(n, slot, half, kept, received, t_high, t_low, base_high, base_low):
    final = t_high.shape[0] - 1
    last = split(dot3((t_high[final], t_low[final]), stacked(n, half, kept, received)))
    return dot3((base_high[slot], base_low[slot]), last, 0)


def finished(slot, half, kept, received, t_high, t_low, base_high, base_low, near):
    return near + far_rows(slot, slot, half, kept, received, t_high, t_low, base_high, base_low)


def turn_body(leaf, slot, near, kept, received, t_high, t_low, base_high, base_low, next_kept, next_send, once):
    half, size = t_high.shape[1] // 2, base_high.shape[2]
    rows = slice(leaf * size, (leaf + 1) * size)
    field = finished(slot, half, kept, received, t_high, t_low, base_high, base_low, near[rows])
    once[...] = field
    store_halves(0, dot3((base_high[slot], base_low[slot]), split(field)), next_kept, next_send)


def edge_turn_body(leaf, slot, names, parity, *refs):
    given, (*refs, across) = dict(zip(names, refs)), refs[len(names) :]
    turn_body(leaf, slot, *refs)
    once = refs[-1]
    first, last = given.get("first", once), given.get("last", once)
    edges(parity, first[:HALO], last[last.shape[0] - HALO :], refs[-2], across)


def turn(line, leaf, slot, near, end, trans, base, edge, cost):
    half, size, columns = trans[0].shape[1] // 2, base[0].shape[2], near.shape[1]
    ins = [(VMEM, a) for a in (near, *end, *trans, *base)]
    outs = [(VMEM, ((half + (HALO if edge else 0), columns), F32)), (VMEM, ((size, columns), F32))]
    outs = [(VMEM, ((half, columns), F32))] + outs
    body = functools.partial(turn_body, leaf, slot)
    if edge:
        parity, given = edge
        body = functools.partial(edge_turn_body, leaf, slot, tuple(given))
        ins = [(SMEM, parity)] + [(VMEM, a) for a in given.values()] + ins
        outs.append((VMEM, ((HALO, columns), F32)))
    return line.call(body, ins, outs, cost=cost)


def far_body(slot, kept, received, t_high, t_low, base_high, base_low, far):
    far[...] = far_rows(0, slot, t_high.shape[1] // 2, kept, received, t_high, t_low, base_high, base_low)


def far_field(line, slot, end, trans, base, cost):
    shape = (base[0].shape[2], end[0].shape[1])
    return line.call(
        functools.partial(far_body, slot),
        [(VMEM, a) for a in (*end, *trans, *base)],
        [(VMEM, (shape, F32))],
        cost=cost,
    )[0]


def put(copies, value, start, buf, out, sems):
    n = len(copies)
    buf[n] = value
    copies.append(pltpu.make_async_copy(buf.at[n], out.at[pl.ds(start, buf.shape[1])], sems.at[n]))
    copies[-1].start()


def near_again_body(parts, done, rest, parity, near_edge, far_edge, *refs):
    fields, refs = refs[:parts], refs[parts:]
    (band_high, band_low), fars = refs[:2], refs[2 : 2 + len(done)]
    out, near, buf, result, sems = refs[2 + len(done) :]
    extend(parity, near_edge, far_edge, fields, buf)
    size = near.shape[0] // len(rest)
    per = size // STRIP
    copies = []
    for leaf, far in zip(done, fars):
        strips = [strip_product(band_high, band_low, leaf * per + s, buf) for s in range(per)]
        put(copies, jnp.concatenate(strips, axis=0) + far[...], leaf * size, result, out, sems)
    for n, leaf in enumerate(rest):
        for s in range(per):
            at = n * size + s * STRIP
            near[at : at + STRIP] = strip_product(band_high, band_low, leaf * per + s, buf)
    for copy in copies:
        copy.wait()


def near_again(line, parity, fields, halo, band, fars, rest, cost):
    size, columns = fields[0].shape
    rows = size * len(fields)
    return line.call(
        functools.partial(near_again_body, len(fields), tuple(fars), rest),
        [(SMEM, parity)] + [(VMEM, a) for a in (*halo, *fields, *band, *fars.values())],
        [(HBM, ((rows, columns), F32)), (VMEM, ((len(rest) * size, columns), F32))],
        [
            pltpu.VMEM((2, rows + 2 * HALO, columns), BF16),
            pltpu.VMEM((len(fars), size, columns), F32),
            pltpu.SemaphoreType.DMA((len(fars),)),
        ],
        cost=cost,
    )


def tail_body(leaf, place, slot, near, kept, received, t_high, t_low, base_high, base_low, _, out, buf, sems):
    half, size = t_high.shape[1] // 2, base_high.shape[2]
    far = far_rows(0, slot, half, kept, received, t_high, t_low, base_high, base_low)
    copies = []
    put(copies, near[place * size : (place + 1) * size] + far, leaf * size, buf, out, sems)
    copies[0].wait()


def tail(line, leaf, place, slot, near, end, trans, base, out, cost):
    size = base[0].shape[2]
    return line.call(
        functools.partial(tail_body, leaf, place, slot),
        [(VMEM, a) for a in (near, *end, *trans, *base)] + [(HBM, out)],
        [(HBM, (out.shape, F32))],
        [pltpu.VMEM((1, size, near.shape[1]), F32), pltpu.SemaphoreType.DMA((1,))],
        aliases={7: 0},
        cost=cost,
    )[0]


def partner(value, level, count):
    return lax.ppermute(value, "block", [(i, i ^ 2**level) for i in range(count)])


def other_side(edge, count):
    pairs = [(i, i + 1) for i in range(1, count - 1, 2)]
    return lax.ppermute(edge, "block", pairs + [(b, a) for a, b in pairs])


COST = {"H": 0.7, "P": 1.0, "h": 0.02, "B": 2.5, "N": 1.0, "T": 0.7, "g": 1.0, "F": 0.02, "A": 1.5, "E": 0.02}
TWO_LEVELS = "H0 H1 h0 H2 B h1 H3 h2 N T0 h3 T1 g0 T2 g1 T3 F0 g2 F1 g3 A E2 E3"


def plan(leaves, levels):
    ends = (0, leaves - 1)
    inside = tuple(range(1, leaves - 1))
    if levels == 2 and leaves == 4:
        order = [(step[0], 0, int(step[1:] or 0)) for step in TWO_LEVELS.split()]
        return [(leaf,) for leaf in ends + inside], ends + inside, order
    stages = [("H", 0)] + [("h", level) for level in range(levels - 1)] + [("T", 0)]
    stages += [("g", level) for level in range(levels - 1)] + [("E", 0)]
    timed = sorted(
        (2 * s + c, -s, kind, level, c) for c in range(leaves) for s, (kind, level) in enumerate(stages)
    )
    order = []
    for _, _, kind, level, c in timed:
        if kind == "T" and c == 0:
            order += [("B", 0, 0), ("N", 0, 0)]
        if kind == "E" and c < 2:
            kind = "F"
        if kind == "E" and c == 2:
            order.append(("A", 0, 0))
        order.append((kind, level, c))
    turns = ends + inside
    return [(leaf,) for leaf in turns], turns, order


def per_device(x, bases, trans, order, offsets, coef):
    count = lax.axis_size("block")
    leaves, levels = bases.shape[0], count.bit_length() - 1
    chunks, turns, steps = plan(leaves, levels)
    home = {leaf: (c, chunk.index(leaf)) for c, chunk in enumerate(chunks) for leaf in chunk}
    parity = jnp.reshape(lax.axis_index("block") % 2, (1,)).astype(jnp.int32)
    line = Line()
    state, base, ends, once, fars = {}, {}, {}, {}, {}
    moves = band = near = out = None
    for kind, level, c in steps:
        cost = COST[kind]
        if kind == "H":
            if c == 0:
                kept, send, *base[c], across, x, bases = first_head(line, chunks[0], parity, order, x, bases, cost)
            else:
                kept, send, *base[c] = head(line, chunks[c], order, x, bases, cost)
            state[c] = kept, partner(send, 0, count)
            if c == 0:
                halo = state[c][1], other_side(across, count)
        elif kind == "h":
            if moves is None:
                moves = trans_prep(line, order, trans, COST["P"])
            kept, send = hop(line, level, len(chunks[c]), *state[c], moves, cost)
            state[c] = kept, partner(send, level + 1, count)
        elif kind == "B":
            band = band_prep(line, offsets, coef, cost)
        elif kind == "N":
            near = near_field(line, parity, x, halo, band, cost)
        elif kind == "T":
            leaf = turns[c]
            chunk, slot = home[leaf]
            edge = None
            if c == 1:
                edge = parity, {name: once[at] for name, at in (("first", 0), ("last", leaves - 1)) if at in once}
            kept, send, once[leaf], *across = turn(
                line, leaf, slot, near, state[chunk], moves, base[chunk], edge, cost
            )
            ends[c] = kept, partner(send, 0, count)
            if c == 1:
                halo = ends[c][1], other_side(across[0], count)
        elif kind == "g":
            kept, send = hop(line, level, 1, *ends[c], moves, cost)
            ends[c] = kept, partner(send, level + 1, count)
        elif kind == "F":
            chunk, slot = home[turns[c]]
            fars[turns[c]] = far_field(line, slot, ends[c], moves, base[chunk], cost)
        elif kind == "A":
            rest = tuple(leaf for leaf in turns if leaf not in fars)
            fields = [once[leaf] for leaf in range(leaves)]
            out, near = near_again(line, parity, fields, halo, band, fars, rest, cost)
        else:
            leaf = turns[c]
            chunk, slot = home[leaf]
            out = tail(line, leaf, rest.index(leaf), slot, near, ends[c], moves, base[chunk], out, cost)
    return out


def solution(mesh):
    in_specs = (
        P("block", ("groups", "exc", "sub")),
        P("block", None, None),
        P(),
        P(),
        P(),
        P(None, "block"),
    )
    out_specs = P("block", ("groups", "exc", "sub"))
    return jax.shard_map(
        per_device, mesh=mesh, in_specs=in_specs, out_specs=out_specs, check_vma=False
    )
```

```python
import functools

import jax
import jax.numpy as jnp
from jax import lax
from jax.experimental import pallas as pl
from jax.experimental.pallas import tpu as pltpu
from jax.sharding import PartitionSpec as P

HALO = 64
STRIP = 128
F32 = jnp.float32
BF16 = jnp.bfloat16
LIMIT = 16 * 1024 * 1024

VMEM = pl.BlockSpec(memory_space=pltpu.VMEM)
SMEM = pl.BlockSpec(memory_space=pltpu.SMEM)
HBM = pl.BlockSpec(memory_space=pltpu.HBM)


class Line:
    def __init__(self):
        self.last = None

    def call(self, body, ins, outs, scratch=(), aliases=None, cost=1.0):
        values = [a for _, a in ins]
        if self.last is not None:
            *values, _ = lax.optimization_barrier((*values, self.last))
        placed = [
            a if s is SMEM else pltpu.with_memory_space_constraint(a, s.memory_space)
            for (s, _), a in zip(ins, values)
        ]
        result = pl.pallas_call(
            body,
            in_specs=[s for s, _ in ins],
            out_specs=[s for s, _ in outs],
            out_shape=[s.memory_space(*shape) for s, shape in outs],
            scratch_shapes=list(scratch),
            input_output_aliases=aliases or {},
            compiler_params=pltpu.CompilerParams(vmem_limit_bytes=LIMIT),
            cost_estimate=pl.CostEstimate(
                flops=int(cost * 1e9), bytes_accessed=int(cost * 3e6), transcendentals=0
            ),
        )(*placed)
        self.last = result[0]
        return result


def split(value):
    high = value.astype(BF16)
    return high, (value - high.astype(F32)).astype(BF16)


def dot(a, b, a_dim=1):
    return lax.dot_general(a, b, (((a_dim,), (0,)), ((), ())), preferred_element_type=F32)


def dot3(a, b, a_dim=1):
    return dot(a[0], b[0], a_dim) + (dot(a[0], b[1], a_dim) + dot(a[1], b[0], a_dim))


def picker(order_ref, level, rank):
    row = order_ref[pl.ds(level, 1), :]
    where = lax.broadcasted_iota(jnp.int32, (rank, rank), 0)
    return jnp.where(where == row, 1.0, 0.0).astype(BF16)


def pick(chosen, pair):
    return tuple(dot(chosen, part, 0).astype(BF16) for part in pair)


def store_halves(n, result, kept, send):
    half = result.shape[0] // 2
    kept[n * half : (n + 1) * half] = result[:half]
    send[n * half : (n + 1) * half] = result[half:]


def stacked(n, half, kept, received):
    rows = slice(n * half, (n + 1) * half)
    return split(jnp.concatenate([kept[rows], received[rows]], axis=0))


def head_leaves(n, base, x, kept, send, base_high, base_low):
    base_high[n], base_low[n] = base
    store_halves(n, dot3(base, split(x)), kept, send)


def first_body(leaves, parity, order, x, bases, kept, send, base_high, base_low, across, x_all, bases_all, order_buf, sems):
    _, rank, size = bases.shape
    count = len(leaves)
    ahead, behind = pl.ds(0, count), pl.ds(count, bases.shape[0] - count)
    x_ahead, x_behind = pl.ds(0, count * size), pl.ds(count * size, x.shape[0] - count * size)
    copies = [
        pltpu.make_async_copy(source, target, sems.at[n])
        for n, (source, target) in enumerate(
            (
                (order, order_buf),
                (bases.at[ahead], bases_all.at[ahead]),
                (x.at[x_ahead], x_all.at[x_ahead]),
                (x.at[x_behind], x_all.at[x_behind]),
                (bases.at[behind], bases_all.at[behind]),
            )
        )
    ]
    for copy in copies:
        copy.start()
    copies[0].wait()
    chosen = picker(order_buf, 0, rank)
    copies[1].wait()
    picked = [pick(chosen, split(bases_all[leaf])) for leaf in leaves]
    copies[2].wait()
    for n, leaf in enumerate(leaves):
        head_leaves(n, picked[n], x_all[leaf * size : (leaf + 1) * size], kept, send, base_high, base_low)
    copies[3].wait()
    edges(parity, x_all[:HALO], x_all[x.shape[0] - HALO :], send, across)
    copies[4].wait()


def edges(parity, first, last, send, across):
    even = jnp.full(first.shape, parity[0], jnp.int32) == 0
    send[send.shape[0] - HALO :] = jnp.where(even, last, first)
    across[...] = jnp.where(even, first, last)


def head_body(leaves, order, x, bases, kept, send, base_high, base_low):
    _, rank, size = bases.shape
    chosen = picker(order, 0, rank)
    for n, leaf in enumerate(leaves):
        base = pick(chosen, split(bases[leaf]))
        head_leaves(n, base, x[leaf * size : (leaf + 1) * size], kept, send, base_high, base_low)


def head_outs(leaves, x, bases, extra):
    _, rank, size = bases.shape
    half = len(leaves) * rank // 2
    base = ((len(leaves), rank, size), BF16)
    return [
        (VMEM, ((half, x.shape[1]), F32)),
        (VMEM, ((half + extra, x.shape[1]), F32)),
        (VMEM, base),
        (VMEM, base),
    ]


def first_head(line, leaves, parity, order, x, bases, cost):
    return line.call(
        functools.partial(first_body, leaves),
        [(SMEM, parity), (HBM, order), (HBM, x), (HBM, bases)],
        head_outs(leaves, x, bases, HALO)
        + [(VMEM, ((HALO, x.shape[1]), F32)), (VMEM, (x.shape, F32)), (VMEM, (bases.shape, F32))],
        [pltpu.VMEM(order.shape, jnp.int32), pltpu.SemaphoreType.DMA((5,))],
        cost=cost,
    )


def head(line, leaves, order, x, bases, cost):
    return line.call(
        functools.partial(head_body, leaves),
        [(VMEM, order), (VMEM, x), (VMEM, bases)],
        head_outs(leaves, x, bases, 0),
        cost=cost,
    )


def trans_body(order, trans, out_high, out_low):
    levels, rank, _ = trans.shape
    for level in range(levels):
        chosen = picker(order, (level + 1) % levels, rank)
        out_high[level], out_low[level] = pick(chosen, split(trans[level]))


def trans_prep(line, order, trans, cost):
    shape = (trans.shape, BF16)
    return line.call(trans_body, [(VMEM, order), (VMEM, trans)], [(VMEM, shape), (VMEM, shape)], cost=cost)


def hop_body(level, count, kept, received, t_high, t_low, next_kept, next_send):
    half = kept.shape[0] // count
    for n in range(count):
        result = dot3((t_high[level], t_low[level]), stacked(n, half, kept, received))
        store_halves(n, result, next_kept, next_send)


def hop(line, level, count, kept, received, trans, cost):
    return line.call(
        functools.partial(hop_body, level, count),
        [(VMEM, kept), (VMEM, received), (VMEM, trans[0]), (VMEM, trans[1])],
        [(VMEM, (kept.shape, F32)), (VMEM, (kept.shape, F32))],
        cost=cost,
    )


def band_body(offsets, coef, high, low):
    strips, width, rows = high.shape
    bands, step = coef.shape[0], 16
    apart = lax.broadcasted_iota(jnp.int32, (step, rows), 0) - lax.broadcasted_iota(
        jnp.int32, (step, rows), 1
    )
    for s in range(strips):
        values = [
            jnp.broadcast_to(coef[b : b + 1, s * rows : (s + 1) * rows], (step, rows)) for b in range(bands)
        ]
        for at in range(0, width, step):
            strip = jnp.zeros((step, rows), F32)
            for b in range(bands):
                strip = jnp.where(apart == offsets[b] + (HALO - at), values[b], strip)
            high[s, at : at + step], low[s, at : at + step] = split(strip)


def band_prep(line, offsets, coef, cost):
    shape = ((coef.shape[1] // STRIP, STRIP + 2 * HALO, STRIP), BF16)
    return line.call(band_body, [(SMEM, offsets), (VMEM, coef)], [(VMEM, shape), (VMEM, shape)], cost=cost)


def extend(parity, near_edge, far_edge, fields, buf):
    at = HALO
    for field in fields:
        rows = slice(at, at + field.shape[0])
        buf[0, rows], buf[1, rows] = split(field[...])
        at += field.shape[0]
    from_partner, from_other = near_edge[near_edge.shape[0] - HALO :], far_edge[...]
    even = jnp.full(from_other.shape, parity[0], jnp.int32) == 0
    buf[0, :HALO], buf[1, :HALO] = split(jnp.where(even, from_other, from_partner))
    buf[0, at:], buf[1, at:] = split(jnp.where(even, from_partner, from_other))


def strip_product(band_high, band_low, s, buf):
    rows = slice(s * STRIP, s * STRIP + band_high.shape[1])
    return dot3((band_high[s], band_low[s]), (buf[0, rows], buf[1, rows]), 0)


def near_body(parity, near_edge, far_edge, field, band_high, band_low, near, buf):
    extend(parity, near_edge, far_edge, [field], buf)
    for s in range(band_high.shape[0]):
        near[s * STRIP : (s + 1) * STRIP] = strip_product(band_high, band_low, s, buf)


def near_field(line, parity, field, halo, band, cost):
    rows, columns = field.shape
    return line.call(
        near_body,
        [(SMEM, parity)] + [(VMEM, a) for a in (*halo, field, *band)],
        [(VMEM, ((rows, columns), F32))],
        [pltpu.VMEM((2, rows + 2 * HALO, columns), BF16)],
        cost=cost,
    )[0]


def far_rows(n, slot, half, kept, received, t_high, t_low, base_high, base_low):
    final = t_high.shape[0] - 1
    last = split(dot3((t_high[final], t_low[final]), stacked(n, half, kept, received)))
    return dot3((base_high[slot], base_low[slot]), last, 0)


def finished(slot, half, kept, received, t_high, t_low, base_high, base_low, near):
    return near + far_rows(slot, slot, half, kept, received, t_high, t_low, base_high, base_low)


def turn_body(leaf, slot, near, kept, received, t_high, t_low, base_high, base_low, next_kept, next_send, once):
    half, size = t_high.shape[1] // 2, base_high.shape[2]
    rows = slice(leaf * size, (leaf + 1) * size)
    field = finished(slot, half, kept, received, t_high, t_low, base_high, base_low, near[rows])
    once[...] = field
    store_halves(0, dot3((base_high[slot], base_low[slot]), split(field)), next_kept, next_send)


def edge_turn_body(leaf, slot, names, parity, *refs):
    given, (*refs, across) = dict(zip(names, refs)), refs[len(names) :]
    turn_body(leaf, slot, *refs)
    once = refs[-1]
    first, last = given.get("first", once), given.get("last", once)
    edges(parity, first[:HALO], last[last.shape[0] - HALO :], refs[-2], across)


def turn(line, leaf, slot, near, end, trans, base, edge, cost):
    half, size, columns = trans[0].shape[1] // 2, base[0].shape[2], near.shape[1]
    ins = [(VMEM, a) for a in (near, *end, *trans, *base)]
    outs = [(VMEM, ((half + (HALO if edge else 0), columns), F32)), (VMEM, ((size, columns), F32))]
    outs = [(VMEM, ((half, columns), F32))] + outs
    body = functools.partial(turn_body, leaf, slot)
    if edge:
        parity, given = edge
        body = functools.partial(edge_turn_body, leaf, slot, tuple(given))
        ins = [(SMEM, parity)] + [(VMEM, a) for a in given.values()] + ins
        outs.append((VMEM, ((HALO, columns), F32)))
    return line.call(body, ins, outs, cost=cost)


def far_body(slot, kept, received, t_high, t_low, base_high, base_low, far):
    far[...] = far_rows(0, slot, t_high.shape[1] // 2, kept, received, t_high, t_low, base_high, base_low)


def far_field(line, slot, end, trans, base, cost):
    shape = (base[0].shape[2], end[0].shape[1])
    return line.call(
        functools.partial(far_body, slot),
        [(VMEM, a) for a in (*end, *trans, *base)],
        [(VMEM, (shape, F32))],
        cost=cost,
    )[0]


def put(copies, value, start, buf, out, sems):
    n = len(copies)
    buf[n] = value
    copies.append(pltpu.make_async_copy(buf.at[n], out.at[pl.ds(start, buf.shape[1])], sems.at[n]))
    copies[-1].start()


def near_again_body(parts, done, rest, parity, near_edge, far_edge, *refs):
    fields, refs = refs[:parts], refs[parts:]
    (band_high, band_low), fars = refs[:2], refs[2 : 2 + len(done)]
    out, near, buf, result, sems = refs[2 + len(done) :]
    extend(parity, near_edge, far_edge, fields, buf)
    size = near.shape[0] // len(rest)
    per = size // STRIP
    copies = []
    for leaf, far in zip(done, fars):
        strips = [strip_product(band_high, band_low, leaf * per + s, buf) for s in range(per)]
        put(copies, jnp.concatenate(strips, axis=0) + far[...], leaf * size, result, out, sems)
    for n, leaf in enumerate(rest):
        for s in range(per):
            at = n * size + s * STRIP
            near[at : at + STRIP] = strip_product(band_high, band_low, leaf * per + s, buf)
    for copy in copies:
        copy.wait()


def near_again(line, parity, fields, halo, band, fars, rest, cost):
    size, columns = fields[0].shape
    rows = size * len(fields)
    return line.call(
        functools.partial(near_again_body, len(fields), tuple(fars), rest),
        [(SMEM, parity)] + [(VMEM, a) for a in (*halo, *fields, *band, *fars.values())],
        [(HBM, ((rows, columns), F32)), (VMEM, ((len(rest) * size, columns), F32))],
        [
            pltpu.VMEM((2, rows + 2 * HALO, columns), BF16),
            pltpu.VMEM((len(fars), size, columns), F32),
            pltpu.SemaphoreType.DMA((len(fars),)),
        ],
        cost=cost,
    )


def tail_body(leaf, place, slot, near, kept, received, t_high, t_low, base_high, base_low, _, out, buf, sems):
    half, size = t_high.shape[1] // 2, base_high.shape[2]
    far = far_rows(0, slot, half, kept, received, t_high, t_low, base_high, base_low)
    copies = []
    put(copies, near[place * size : (place + 1) * size] + far, leaf * size, buf, out, sems)
    copies[0].wait()


def tail(line, leaf, place, slot, near, end, trans, base, out, cost):
    size = base[0].shape[2]
    return line.call(
        functools.partial(tail_body, leaf, place, slot),
        [(VMEM, a) for a in (near, *end, *trans, *base)] + [(HBM, out)],
        [(HBM, (out.shape, F32))],
        [pltpu.VMEM((1, size, near.shape[1]), F32), pltpu.SemaphoreType.DMA((1,))],
        aliases={7: 0},
        cost=cost,
    )[0]


def partner(value, level, count):
    return lax.ppermute(value, "block", [(i, i ^ 2**level) for i in range(count)])


def other_side(edge, count):
    pairs = [(i, i + 1) for i in range(1, count - 1, 2)]
    return lax.ppermute(edge, "block", pairs + [(b, a) for a, b in pairs])


COST = {"H": 0.7, "P": 1.0, "h": 0.02, "B": 2.5, "N": 1.0, "T": 0.7, "g": 1.0, "F": 0.02, "A": 1.5, "E": 0.02}
HEADS = ("H0", "H1", "h0", "H2", "B", "h1", "H3", "N", "h2")
TURNS = ("T0", "h3", "T1", "g0", "T2", "g1", "T3", "F0", "g2", "F1", "g3")
ENDS = ("A", "E2", "E3")


def plan(leaves, levels):
    ends = (0, leaves - 1)
    inside = tuple(range(1, leaves - 1))
    if levels == 2 and leaves == 4:
        order = [(step[0], 0, int(step[1:] or 0)) for step in HEADS + TURNS + ENDS]
        return [(leaf,) for leaf in ends + inside], ends + inside, order
    stages = [("H", 0)] + [("h", level) for level in range(levels - 1)] + [("T", 0)]
    stages += [("g", level) for level in range(levels - 1)] + [("E", 0)]
    timed = sorted(
        (2 * s + c, -s, kind, level, c) for c in range(leaves) for s, (kind, level) in enumerate(stages)
    )
    order = []
    for _, _, kind, level, c in timed:
        if kind == "T" and c == 0:
            order += [("B", 0, 0), ("N", 0, 0)]
        if kind == "E" and c < 2:
            kind = "F"
        if kind == "E" and c == 2:
            order.append(("A", 0, 0))
        order.append((kind, level, c))
    turns = ends + inside
    return [(leaf,) for leaf in turns], turns, order


def per_device(x, bases, trans, order, offsets, coef):
    count = lax.axis_size("block")
    leaves, levels = bases.shape[0], count.bit_length() - 1
    chunks, turns, steps = plan(leaves, levels)
    home = {leaf: (c, chunk.index(leaf)) for c, chunk in enumerate(chunks) for leaf in chunk}
    parity = jnp.reshape(lax.axis_index("block") % 2, (1,)).astype(jnp.int32)
    line = Line()
    state, base, ends, once, fars = {}, {}, {}, {}, {}
    moves = band = near = out = None
    for kind, level, c in steps:
        cost = COST[kind]
        if kind == "H":
            if c == 0:
                kept, send, *base[c], across, x, bases = first_head(line, chunks[0], parity, order, x, bases, cost)
            else:
                kept, send, *base[c] = head(line, chunks[c], order, x, bases, cost)
            state[c] = kept, partner(send, 0, count)
            if c == 0:
                halo = state[c][1], other_side(across, count)
        elif kind == "h":
            if moves is None:
                moves = trans_prep(line, order, trans, COST["P"])
            kept, send = hop(line, level, len(chunks[c]), *state[c], moves, cost)
            state[c] = kept, partner(send, level + 1, count)
        elif kind == "B":
            band = band_prep(line, offsets, coef, cost)
        elif kind == "N":
            near = near_field(line, parity, x, halo, band, cost)
        elif kind == "T":
            leaf = turns[c]
            chunk, slot = home[leaf]
            edge = None
            if c == 1:
                edge = parity, {name: once[at] for name, at in (("first", 0), ("last", leaves - 1)) if at in once}
            kept, send, once[leaf], *across = turn(
                line, leaf, slot, near, state[chunk], moves, base[chunk], edge, cost
            )
            ends[c] = kept, partner(send, 0, count)
            if c == 1:
                halo = ends[c][1], other_side(across[0], count)
        elif kind == "g":
            kept, send = hop(line, level, 1, *ends[c], moves, cost)
            ends[c] = kept, partner(send, level + 1, count)
        elif kind == "F":
            chunk, slot = home[turns[c]]
            fars[turns[c]] = far_field(line, slot, ends[c], moves, base[chunk], cost)
        elif kind == "A":
            rest = tuple(leaf for leaf in turns if leaf not in fars)
            fields = [once[leaf] for leaf in range(leaves)]
            out, near = near_again(line, parity, fields, halo, band, fars, rest, cost)
        else:
            leaf = turns[c]
            chunk, slot = home[leaf]
            out = tail(line, leaf, rest.index(leaf), slot, near, ends[c], moves, base[chunk], out, cost)
    return out


def solution(mesh):
    in_specs = (
        P("block", ("groups", "exc", "sub")),
        P("block", None, None),
        P(),
        P(),
        P(),
        P(None, "block"),
    )
    out_specs = P("block", ("groups", "exc", "sub"))
    return jax.shard_map(
        per_device, mesh=mesh, in_specs=in_specs, out_specs=out_specs, check_vma=False
    )
```

```python
import functools

import jax
import jax.numpy as jnp
from jax import lax
from jax.experimental import pallas as pl
from jax.experimental.pallas import tpu as pltpu
from jax.sharding import PartitionSpec as P

HALO = 64
STRIP = 128
F32 = jnp.float32
BF16 = jnp.bfloat16
LIMIT = 16 * 1024 * 1024

VMEM = pl.BlockSpec(memory_space=pltpu.VMEM)
SMEM = pl.BlockSpec(memory_space=pltpu.SMEM)
HBM = pl.BlockSpec(memory_space=pltpu.HBM)


class Line:
    def __init__(self):
        self.last = None

    def call(self, body, ins, outs, scratch=(), aliases=None, cost=1.0):
        values = [a for _, a in ins]
        if self.last is not None:
            *values, _ = lax.optimization_barrier((*values, self.last))
        placed = [
            a if s is SMEM else pltpu.with_memory_space_constraint(a, s.memory_space)
            for (s, _), a in zip(ins, values)
        ]
        result = pl.pallas_call(
            body,
            in_specs=[s for s, _ in ins],
            out_specs=[s for s, _ in outs],
            out_shape=[s.memory_space(*shape) for s, shape in outs],
            scratch_shapes=list(scratch),
            input_output_aliases=aliases or {},
            compiler_params=pltpu.CompilerParams(vmem_limit_bytes=LIMIT),
            cost_estimate=pl.CostEstimate(
                flops=int(cost * 1e9), bytes_accessed=int(cost * 3e6), transcendentals=0
            ),
        )(*placed)
        self.last = result[0]
        return result


def split(value):
    high = value.astype(BF16)
    return high, (value - high.astype(F32)).astype(BF16)


def dot(a, b, a_dim=1):
    return lax.dot_general(a, b, (((a_dim,), (0,)), ((), ())), preferred_element_type=F32)


def dot3(a, b, a_dim=1):
    return dot(a[0], b[0], a_dim) + (dot(a[0], b[1], a_dim) + dot(a[1], b[0], a_dim))


def picker(order_ref, level, rank):
    row = order_ref[pl.ds(level, 1), :]
    where = lax.broadcasted_iota(jnp.int32, (rank, rank), 0)
    return jnp.where(where == row, 1.0, 0.0).astype(BF16)


def pick(chosen, pair):
    return tuple(dot(chosen, part, 0).astype(BF16) for part in pair)


def store_halves(n, result, kept, send):
    half = result.shape[0] // 2
    kept[n * half : (n + 1) * half] = result[:half]
    send[n * half : (n + 1) * half] = result[half:]


def stacked(n, half, kept, received):
    rows = slice(n * half, (n + 1) * half)
    return split(jnp.concatenate([kept[rows], received[rows]], axis=0))


def head_leaves(n, base, x, kept, send, base_high, base_low):
    base_high[n], base_low[n] = base
    store_halves(n, dot3(base, split(x)), kept, send)


def first_body(leaves, parity, order, x, bases, kept, send, base_high, base_low, across, x_all, bases_all, order_buf, sems):
    _, rank, size = bases.shape
    count = len(leaves)
    ahead, behind = pl.ds(0, count), pl.ds(count, bases.shape[0] - count)
    x_ahead, x_behind = pl.ds(0, count * size), pl.ds(count * size, x.shape[0] - count * size)
    copies = [
        pltpu.make_async_copy(source, target, sems.at[n])
        for n, (source, target) in enumerate(
            (
                (order, order_buf),
                (bases.at[ahead], bases_all.at[ahead]),
                (x.at[x_ahead], x_all.at[x_ahead]),
                (x.at[x_behind], x_all.at[x_behind]),
                (bases.at[behind], bases_all.at[behind]),
            )
        )
    ]
    for copy in copies:
        copy.start()
    copies[0].wait()
    chosen = picker(order_buf, 0, rank)
    copies[1].wait()
    picked = [pick(chosen, split(bases_all[leaf])) for leaf in leaves]
    copies[2].wait()
    for n, leaf in enumerate(leaves):
        head_leaves(n, picked[n], x_all[leaf * size : (leaf + 1) * size], kept, send, base_high, base_low)
    copies[3].wait()
    edges(parity, x_all[:HALO], x_all[x.shape[0] - HALO :], send, across)
    copies[4].wait()


def edges(parity, first, last, send, across):
    even = jnp.full(first.shape, parity[0], jnp.int32) == 0
    send[send.shape[0] - HALO :] = jnp.where(even, last, first)
    across[...] = jnp.where(even, first, last)


def head_body(leaves, order, x, bases, kept, send, base_high, base_low):
    _, rank, size = bases.shape
    chosen = picker(order, 0, rank)
    for n, leaf in enumerate(leaves):
        base = pick(chosen, split(bases[leaf]))
        head_leaves(n, base, x[leaf * size : (leaf + 1) * size], kept, send, base_high, base_low)


def head_outs(leaves, x, bases, extra):
    _, rank, size = bases.shape
    half = len(leaves) * rank // 2
    base = ((len(leaves), rank, size), BF16)
    return [
        (VMEM, ((half, x.shape[1]), F32)),
        (VMEM, ((half + extra, x.shape[1]), F32)),
        (VMEM, base),
        (VMEM, base),
    ]


def first_head(line, leaves, parity, order, x, bases, cost):
    return line.call(
        functools.partial(first_body, leaves),
        [(SMEM, parity), (HBM, order), (HBM, x), (HBM, bases)],
        head_outs(leaves, x, bases, HALO)
        + [(VMEM, ((HALO, x.shape[1]), F32)), (VMEM, (x.shape, F32)), (VMEM, (bases.shape, F32))],
        [pltpu.VMEM(order.shape, jnp.int32), pltpu.SemaphoreType.DMA((5,))],
        cost=cost,
    )


def head(line, leaves, order, x, bases, cost):
    return line.call(
        functools.partial(head_body, leaves),
        [(VMEM, order), (VMEM, x), (VMEM, bases)],
        head_outs(leaves, x, bases, 0),
        cost=cost,
    )


def trans_body(order, trans, out_high, out_low):
    levels, rank, _ = trans.shape
    for level in range(levels):
        chosen = picker(order, (level + 1) % levels, rank)
        out_high[level], out_low[level] = pick(chosen, split(trans[level]))


def trans_prep(line, order, trans, cost):
    shape = (trans.shape, BF16)
    return line.call(trans_body, [(VMEM, order), (VMEM, trans)], [(VMEM, shape), (VMEM, shape)], cost=cost)


def hop_body(level, count, kept, received, t_high, t_low, next_kept, next_send):
    half = kept.shape[0] // count
    for n in range(count):
        result = dot3((t_high[level], t_low[level]), stacked(n, half, kept, received))
        store_halves(n, result, next_kept, next_send)


def hop(line, level, count, kept, received, trans, cost):
    return line.call(
        functools.partial(hop_body, level, count),
        [(VMEM, kept), (VMEM, received), (VMEM, trans[0]), (VMEM, trans[1])],
        [(VMEM, (kept.shape, F32)), (VMEM, (kept.shape, F32))],
        cost=cost,
    )


def band_body(offsets, coef, high, low):
    strips, width, rows = high.shape
    bands, step = coef.shape[0], 16
    apart = lax.broadcasted_iota(jnp.int32, (step, rows), 0) - lax.broadcasted_iota(
        jnp.int32, (step, rows), 1
    )
    for s in range(strips):
        values = [
            jnp.broadcast_to(coef[b : b + 1, s * rows : (s + 1) * rows], (step, rows)) for b in range(bands)
        ]
        for at in range(0, width, step):
            strip = jnp.zeros((step, rows), F32)
            for b in range(bands):
                strip = jnp.where(apart == offsets[b] + (HALO - at), values[b], strip)
            high[s, at : at + step], low[s, at : at + step] = split(strip)


def band_prep(line, offsets, coef, cost):
    shape = ((coef.shape[1] // STRIP, STRIP + 2 * HALO, STRIP), BF16)
    return line.call(band_body, [(SMEM, offsets), (VMEM, coef)], [(VMEM, shape), (VMEM, shape)], cost=cost)


def extend(parity, near_edge, far_edge, fields, buf):
    at = HALO
    for field in fields:
        rows = slice(at, at + field.shape[0])
        buf[0, rows], buf[1, rows] = split(field[...])
        at += field.shape[0]
    from_partner, from_other = near_edge[near_edge.shape[0] - HALO :], far_edge[...]
    even = jnp.full(from_other.shape, parity[0], jnp.int32) == 0
    buf[0, :HALO], buf[1, :HALO] = split(jnp.where(even, from_other, from_partner))
    buf[0, at:], buf[1, at:] = split(jnp.where(even, from_partner, from_other))


def strip_product(band_high, band_low, s, buf):
    rows = slice(s * STRIP, s * STRIP + band_high.shape[1])
    return dot3((band_high[s], band_low[s]), (buf[0, rows], buf[1, rows]), 0)


def near_body(parity, near_edge, far_edge, field, band_high, band_low, near, buf):
    extend(parity, near_edge, far_edge, [field], buf)
    for s in range(band_high.shape[0]):
        near[s * STRIP : (s + 1) * STRIP] = strip_product(band_high, band_low, s, buf)


def near_field(line, parity, field, halo, band, cost):
    rows, columns = field.shape
    return line.call(
        near_body,
        [(SMEM, parity)] + [(VMEM, a) for a in (*halo, field, *band)],
        [(VMEM, ((rows, columns), F32))],
        [pltpu.VMEM((2, rows + 2 * HALO, columns), BF16)],
        cost=cost,
    )[0]


def far_rows(n, slot, half, kept, received, t_high, t_low, base_high, base_low):
    final = t_high.shape[0] - 1
    last = split(dot3((t_high[final], t_low[final]), stacked(n, half, kept, received)))
    return dot3((base_high[slot], base_low[slot]), last, 0)


def finished(slot, half, kept, received, t_high, t_low, base_high, base_low, near):
    return near + far_rows(slot, slot, half, kept, received, t_high, t_low, base_high, base_low)


def turn_body(leaf, slot, near, kept, received, t_high, t_low, base_high, base_low, next_kept, next_send, once):
    half, size = t_high.shape[1] // 2, base_high.shape[2]
    rows = slice(leaf * size, (leaf + 1) * size)
    field = finished(slot, half, kept, received, t_high, t_low, base_high, base_low, near[rows])
    once[...] = field
    store_halves(0, dot3((base_high[slot], base_low[slot]), split(field)), next_kept, next_send)


def edge_turn_body(leaf, slot, names, parity, *refs):
    given, (*refs, across) = dict(zip(names, refs)), refs[len(names) :]
    turn_body(leaf, slot, *refs)
    once = refs[-1]
    first, last = given.get("first", once), given.get("last", once)
    edges(parity, first[:HALO], last[last.shape[0] - HALO :], refs[-2], across)


def turn(line, leaf, slot, near, end, trans, base, edge, cost):
    half, size, columns = trans[0].shape[1] // 2, base[0].shape[2], near.shape[1]
    ins = [(VMEM, a) for a in (near, *end, *trans, *base)]
    outs = [(VMEM, ((half + (HALO if edge else 0), columns), F32)), (VMEM, ((size, columns), F32))]
    outs = [(VMEM, ((half, columns), F32))] + outs
    body = functools.partial(turn_body, leaf, slot)
    if edge:
        parity, given = edge
        body = functools.partial(edge_turn_body, leaf, slot, tuple(given))
        ins = [(SMEM, parity)] + [(VMEM, a) for a in given.values()] + ins
        outs.append((VMEM, ((HALO, columns), F32)))
    return line.call(body, ins, outs, cost=cost)


def far_body(slot, kept, received, t_high, t_low, base_high, base_low, far):
    far[...] = far_rows(0, slot, t_high.shape[1] // 2, kept, received, t_high, t_low, base_high, base_low)


def far_field(line, slot, end, trans, base, cost):
    shape = (base[0].shape[2], end[0].shape[1])
    return line.call(
        functools.partial(far_body, slot),
        [(VMEM, a) for a in (*end, *trans, *base)],
        [(VMEM, (shape, F32))],
        cost=cost,
    )[0]


def put(copies, value, start, buf, out, sems):
    n = len(copies)
    buf[n] = value
    copies.append(pltpu.make_async_copy(buf.at[n], out.at[pl.ds(start, buf.shape[1])], sems.at[n]))
    copies[-1].start()


def near_again_body(parts, done, rest, parity, near_edge, far_edge, *refs):
    fields, refs = refs[:parts], refs[parts:]
    (band_high, band_low), fars = refs[:2], refs[2 : 2 + len(done)]
    out, near, buf, result, sems = refs[2 + len(done) :]
    extend(parity, near_edge, far_edge, fields, buf)
    size = near.shape[0] // len(rest)
    per = size // STRIP
    copies = []
    for leaf, far in zip(done, fars):
        strips = [strip_product(band_high, band_low, leaf * per + s, buf) for s in range(per)]
        put(copies, jnp.concatenate(strips, axis=0) + far[...], leaf * size, result, out, sems)
    for n, leaf in enumerate(rest):
        for s in range(per):
            at = n * size + s * STRIP
            near[at : at + STRIP] = strip_product(band_high, band_low, leaf * per + s, buf)
    for copy in copies:
        copy.wait()


def near_again(line, parity, fields, halo, band, fars, rest, cost):
    size, columns = fields[0].shape
    rows = size * len(fields)
    return line.call(
        functools.partial(near_again_body, len(fields), tuple(fars), rest),
        [(SMEM, parity)] + [(VMEM, a) for a in (*halo, *fields, *band, *fars.values())],
        [(HBM, ((rows, columns), F32)), (VMEM, ((len(rest) * size, columns), F32))],
        [
            pltpu.VMEM((2, rows + 2 * HALO, columns), BF16),
            pltpu.VMEM((len(fars), size, columns), F32),
            pltpu.SemaphoreType.DMA((len(fars),)),
        ],
        cost=cost,
    )


def tail_body(leaf, place, slot, near, kept, received, t_high, t_low, base_high, base_low, _, out, buf, sems):
    half, size = t_high.shape[1] // 2, base_high.shape[2]
    final, part = t_high.shape[0] - 1, buf.shape[1]
    last = split(dot3((t_high[final], t_low[final]), stacked(0, half, kept, received)))
    copies = []
    for at in range(0, size, part):
        columns = slice(at, at + part)
        far = dot3((base_high[slot, :, columns], base_low[slot, :, columns]), last, 0)
        rows = slice(place * size + at, place * size + at + part)
        put(copies, near[rows] + far, leaf * size + at, buf, out, sems)
    for copy in copies:
        copy.wait()


def tail(line, leaf, place, slot, near, end, trans, base, out, cost):
    size = base[0].shape[2]
    return line.call(
        functools.partial(tail_body, leaf, place, slot),
        [(VMEM, a) for a in (near, *end, *trans, *base)] + [(HBM, out)],
        [(HBM, (out.shape, F32))],
        [pltpu.VMEM((2, size // 2, near.shape[1]), F32), pltpu.SemaphoreType.DMA((2,))],
        aliases={7: 0},
        cost=cost,
    )[0]


def partner(value, level, count):
    return lax.ppermute(value, "block", [(i, i ^ 2**level) for i in range(count)])


def other_side(edge, count):
    pairs = [(i, i + 1) for i in range(1, count - 1, 2)]
    return lax.ppermute(edge, "block", pairs + [(b, a) for a, b in pairs])


COST = {"H": 0.7, "P": 1.0, "h": 0.02, "B": 2.5, "N": 1.0, "T": 0.7, "g": 1.0, "F": 0.02, "A": 1.5, "E": 0.02}
HEADS = ("H0", "H1", "h0", "H2", "B", "h1", "H3", "N", "h2")
TURNS = ("T0", "h3", "T1", "g0", "T2", "g1", "T3", "F0", "g2", "F1", "g3")
ENDS = ("A", "E2", "E3")


def plan(leaves, levels):
    ends = (0, leaves - 1)
    inside = tuple(range(1, leaves - 1))
    if levels == 2 and leaves == 4:
        order = [(step[0], 0, int(step[1:] or 0)) for step in HEADS + TURNS + ENDS]
        return [(leaf,) for leaf in ends + inside], ends + inside, order
    stages = [("H", 0)] + [("h", level) for level in range(levels - 1)] + [("T", 0)]
    stages += [("g", level) for level in range(levels - 1)] + [("E", 0)]
    timed = sorted(
        (2 * s + c, -s, kind, level, c) for c in range(leaves) for s, (kind, level) in enumerate(stages)
    )
    order = []
    for _, _, kind, level, c in timed:
        if kind == "T" and c == 0:
            order += [("B", 0, 0), ("N", 0, 0)]
        if kind == "E" and c < 2:
            kind = "F"
        if kind == "E" and c == 2:
            order.append(("A", 0, 0))
        order.append((kind, level, c))
    turns = ends + inside
    return [(leaf,) for leaf in turns], turns, order


def per_device(x, bases, trans, order, offsets, coef):
    count = lax.axis_size("block")
    leaves, levels = bases.shape[0], count.bit_length() - 1
    chunks, turns, steps = plan(leaves, levels)
    home = {leaf: (c, chunk.index(leaf)) for c, chunk in enumerate(chunks) for leaf in chunk}
    parity = jnp.reshape(lax.axis_index("block") % 2, (1,)).astype(jnp.int32)
    line = Line()
    state, base, ends, once, fars = {}, {}, {}, {}, {}
    moves = band = near = out = None
    for kind, level, c in steps:
        cost = COST[kind]
        if kind == "H":
            if c == 0:
                kept, send, *base[c], across, x, bases = first_head(line, chunks[0], parity, order, x, bases, cost)
            else:
                kept, send, *base[c] = head(line, chunks[c], order, x, bases, cost)
            state[c] = kept, partner(send, 0, count)
            if c == 0:
                halo = state[c][1], other_side(across, count)
        elif kind == "h":
            if moves is None:
                moves = trans_prep(line, order, trans, COST["P"])
            kept, send = hop(line, level, len(chunks[c]), *state[c], moves, cost)
            state[c] = kept, partner(send, level + 1, count)
        elif kind == "B":
            band = band_prep(line, offsets, coef, cost)
        elif kind == "N":
            near = near_field(line, parity, x, halo, band, cost)
        elif kind == "T":
            leaf = turns[c]
            chunk, slot = home[leaf]
            edge = None
            if c == 1:
                edge = parity, {name: once[at] for name, at in (("first", 0), ("last", leaves - 1)) if at in once}
            kept, send, once[leaf], *across = turn(
                line, leaf, slot, near, state[chunk], moves, base[chunk], edge, cost
            )
            ends[c] = kept, partner(send, 0, count)
            if c == 1:
                halo = ends[c][1], other_side(across[0], count)
        elif kind == "g":
            kept, send = hop(line, level, 1, *ends[c], moves, cost)
            ends[c] = kept, partner(send, level + 1, count)
        elif kind == "F":
            chunk, slot = home[turns[c]]
            fars[turns[c]] = far_field(line, slot, ends[c], moves, base[chunk], cost)
        elif kind == "A":
            rest = tuple(leaf for leaf in turns if leaf not in fars)
            fields = [once[leaf] for leaf in range(leaves)]
            out, near = near_again(line, parity, fields, halo, band, fars, rest, cost)
        else:
            leaf = turns[c]
            chunk, slot = home[leaf]
            out = tail(line, leaf, rest.index(leaf), slot, near, ends[c], moves, base[chunk], out, cost)
    return out


def solution(mesh):
    in_specs = (
        P("block", ("groups", "exc", "sub")),
        P("block", None, None),
        P(),
        P(),
        P(),
        P(None, "block"),
    )
    out_specs = P("block", ("groups", "exc", "sub"))
    return jax.shard_map(
        per_device, mesh=mesh, in_specs=in_specs, out_specs=out_specs, check_vma=False
    )
```
